32 devices in a mesh: cand: 2 (over y), gx: 4 (over z), gy: 2 (over x), ha: 2 (over core).
Axes of the slice: x: 2, y: 2, z: 4, core: 2. Of those that a mesh axis runs over, the one named last changes fastest.
Arguments:
- forward_field: float32 [4, 2, 3, 32, 16, 256], P('ha', None, None, ('cand', 'gx'), 'gy'), parts along dimension 3, may hold values from -4 to 4
- adjoint_source: float32 [4, 2, 3, 32, 16, 256], P('ha', None, None, ('cand', 'gx'), 'gy'), parts along dimension 3, may hold values from -60 to 60
- permittivity: float32 [32, 16, 256], P(('cand', 'gx'), 'gy'), parts along dimension 0, may hold values from 1 to 12
- frequency: float32 [4], replicated, may hold values from 0.1 to 0.35
- design_tiles: int32 [8, 4], P(('cand', 'gx'), 'gy'), parts along dimension 0, may hold values from 0 to 1, as said below
- mix_pairs: int32 [4, 3, 2], replicated, may hold values from 0 to 3
- pml_width: int32 [3], replicated, may hold values from 2 to 5
Outputs:
- adjoint_field: float32 [4, 2, 3, 32, 16, 256], P('ha', None, None, ('cand', 'gx'), 'gy'), parts along dimension 3
- gradient: float32 [32, 16, 256], P(('cand', 'gx'), 'gy'), parts along dimension 0
The draws below stay inside these ranges and needn't reach their ends.
There are 2 independent parts, one for each index of `cand`. The reference program is written for one: setup_inputs(seed, part) draws one part's arguments, and reference() takes and returns one part's arrays. A program takes and returns all parts, laid end to end along the dimension named above; an argument that names none is the same for every part. Nothing has to cross between parts.
Inputs may be any that keep to these rules, and one draw needn't show every extreme that they name: `design_tiles`: 1 marks a design tile of 4 x 4 columns of cells; all ones lie in one rectangle of tiles that spans 1 to 3 devices' widths along x and 1 to 2 along y, and at least one tile is 1. `mix_pairs`: entries name harmonics.
All inputs are finite; a program needn't handle non-finite values.
Results may differ from the reference program's by a relative error of at most 0.0001.
Values sent between devices are 32-bit elements; how exact they have to be, the bound alone decides.
No kernel may reach another device: no remote copies, remote signals or barrier semaphores. Data moves between devices by JAX's collectives and lax.ppermute only.
A program may use at most 64 MiB of HBM per device.

```python
import math
import jax
import jax.numpy as jnp
from jax import lax

HARMONICS = 4
PAIRS = 3
ITERS = 3
TILE = 4
CX = 4
CY = 8
NX = 16
NY = 16
NZ = 256


def draw_design_tiles(key, part):
    key_a, key_b, key_c, key_d, key_e = jax.random.split(jax.random.fold_in(key, 17), 5)
    rows = NX // TILE
    cols = NY // TILE
    span_x = jax.random.randint(key_a, (), CX // TILE, 3 * CX // TILE + 1)
    span_y = jax.random.randint(key_b, (), CY // TILE, 2 * CY // TILE + 1)
    start_x = jax.random.randint(key_c, (), 0, rows - span_x + 1)
    start_y = jax.random.randint(key_d, (), 0, cols - span_y + 1)
    index_x = jnp.arange(rows)[:, None]
    index_y = jnp.arange(cols)[None, :]
    inside = (index_x >= start_x) & (index_x < start_x + span_x) & (index_y >= start_y) & (index_y < start_y + span_y)
    corner = (index_x == start_x) & (index_y == start_y)
    filled = (jax.random.randint(key_e, (rows, cols), 0, 4) > 0) | corner
    return (inside & filled).astype(jnp.int32)


def touch_ends(drawn, own_key, low, top_value):
    extent = drawn.shape
    spot = [jax.random.randint(jax.random.fold_in(own_key, axis), (), 0, extent[axis]) for axis in range(len(extent))]
    drawn = drawn.at[tuple(spot)].set(low)
    longest = extent.index(max(extent))
    spot[longest] = (spot[longest] + 1) % extent[longest]
    return drawn.at[tuple(spot)].set(top_value)


def levels(key, shape, cuts, low, largest):
    factor_of = 1.0
    for axis_at, shards_of in cuts:
        draws = jax.random.uniform(jax.random.fold_in(jax.random.fold_in(key, 6), axis_at), (shards_of,), jnp.float32, low / len(cuts), largest / len(cuts))
        factor_of = factor_of * jnp.repeat(jnp.exp(draws), shape[axis_at] // shards_of).reshape((-1,) + (1,) * (len(shape) - 1 - axis_at))
    return factor_of


def centred(rng, dims, deviation, most, cuts=(), kind=jnp.bfloat16):
    array = deviation * jax.random.normal(rng, dims, jnp.float32)
    if cuts:
        array = array * levels(rng, dims, cuts, -0.22, 0.18)
    return jnp.clip(array, -most, most).astype(kind)


def setup_inputs(seed: int = 0, part: int = 0) -> dict:
    keys = jax.random.split(jax.random.key(seed), 8)
    part_splits = jax.random.split(jax.random.fold_in(keys[7], part), 8)
    forward_field = centred(part_splits[0], (HARMONICS, 2, 3, NX, NY, NZ), 1.0, 4.0, ((0, 2), (3, 4), (4, 2)), jnp.float32)
    adjoint_source = centred(part_splits[1], (HARMONICS, 2, 3, NX, NY, NZ), 10.0, 60.0, ((0, 2), (3, 4), (4, 2)), jnp.float32)
    permittivity = jnp.clip(1.0 + 11.0 * jax.random.uniform(part_splits[2], (NX, NY, NZ), jnp.float32) ** levels(part_splits[2], (NX, NY, NZ), ((0, 4), (1, 2)), -0.2, 0.2), 1.0, 12.0)
    frequency = jnp.clip(jnp.exp(jax.random.uniform(keys[3], (HARMONICS,), jnp.float32, math.log(0.1), math.log(0.35))), 0.1, 0.35)
    design_tiles = draw_design_tiles(jax.random.fold_in(jax.random.fold_in(keys[7], part), 71), part)
    mix_pairs = touch_ends(jax.random.randint(keys[5], (HARMONICS, PAIRS, 2), 0, HARMONICS), jax.random.fold_in(keys[5], 1), 0, HARMONICS - 1).astype(jnp.int32)
    pml_width = jax.random.randint(keys[6], (3,), 2, 6).astype(jnp.int32)
    return {"forward_field": forward_field, "adjoint_source": adjoint_source, "permittivity": permittivity, "frequency": frequency, "design_tiles": design_tiles, "mix_pairs": mix_pairs, "pml_width": pml_width}


kerr_coef = 4.0
sigma_peak = 8.0


def zero_rim(values, along):
    return jnp.zeros_like(lax.slice_in_dim(values, 0, 1, axis=along))


def step_ahead(values, upcoming, along):
    rest = lax.slice_in_dim(values, 1, values.shape[along], axis=along)
    return jnp.concatenate([rest, upcoming], axis=along) - values


def step_behind(values, earlier, along):
    rest = lax.slice_in_dim(values, 0, values.shape[along] - 1, axis=along)
    return values - jnp.concatenate([earlier, rest], axis=along)


def curl_ahead(field_x, field_y, field_z, ahead_x, ahead_y, ahead_z):
    first = field_x.ndim - 3
    second = first + 1
    third = first + 2
    mag_x = step_ahead(field_z, ahead_y[1], second) - step_ahead(field_y, ahead_z[1], third)
    mag_y = step_ahead(field_x, ahead_z[0], third) - step_ahead(field_z, ahead_x[1], first)
    mag_z = step_ahead(field_y, ahead_x[0], first) - step_ahead(field_x, ahead_y[0], second)
    return mag_x, mag_y, mag_z


def curl_behind(mag_x, mag_y, mag_z, behind_x, behind_y, behind_z):
    first = mag_x.ndim - 3
    second = first + 1
    third = first + 2
    out_x = step_behind(mag_z, behind_y[1], second) - step_behind(mag_y, behind_z[1], third)
    out_y = step_behind(mag_x, behind_z[0], third) - step_behind(mag_z, behind_x[1], first)
    out_z = step_behind(mag_y, behind_x[0], first) - step_behind(mag_x, behind_y[0], second)
    return out_x, out_y, out_z


def plain_curl(adjoint):
    field_x = adjoint[:, :, 0]
    field_y = adjoint[:, :, 1]
    field_z = adjoint[:, :, 2]
    first = field_x.ndim - 3
    rim_x = zero_rim(field_x, first)
    rim_y = zero_rim(field_x, first + 1)
    rim_z = zero_rim(field_x, first + 2)
    mag_x, mag_y, mag_z = curl_ahead(field_x, field_y, field_z, (rim_x, rim_x), (rim_y, rim_y), (rim_z, rim_z))
    out_x, out_y, out_z = curl_behind(mag_x, mag_y, mag_z, (rim_x, rim_x), (rim_y, rim_y), (rim_z, rim_z))
    return jnp.stack([out_x, out_y, out_z], axis=2)


def complex_pairs(chosen_field, chosen_adjoint):
    real = jnp.sum(chosen_field[:, :, 0] * chosen_adjoint[:, :, 0] - chosen_field[:, :, 1] * chosen_adjoint[:, :, 1], axis=1)
    imag = jnp.sum(chosen_field[:, :, 0] * chosen_adjoint[:, :, 1] + chosen_field[:, :, 1] * chosen_adjoint[:, :, 0], axis=1)
    return jnp.stack([real, imag], axis=1)


def absorb_profile(width, count, offset, length):
    place = offset + jnp.arange(length, dtype=jnp.int32)
    reach = jnp.maximum(jnp.maximum(width - place, place - (count - 1 - width)), 0)
    return (reach.astype(jnp.float32) / width.astype(jnp.float32)) ** 2


def tiles_to_cells(tiles, tile):
    rows, cols = tiles.shape
    spread = jnp.broadcast_to(tiles[:, None, :, None], (rows, tile, cols, tile))
    return spread.reshape(rows * tile, cols * tile).astype(jnp.float32)[:, :, None]


def reference(forward_field, adjoint_source, permittivity, frequency, design_tiles, mix_pairs, pml_width):
    mask = tiles_to_cells(design_tiles, TILE)
    anchor = jnp.zeros((), jnp.int32)
    sigma = sigma_peak * (absorb_profile(pml_width[0], NX, anchor, NX)[:, None, None]
                          + absorb_profile(pml_width[1], NY, anchor, NY)[None, :, None]
                          + absorb_profile(pml_width[2], NZ, anchor, NZ)[None, None, :])
    squared = frequency * frequency
    weight = squared[:, None, None, None, None, None]
    scale = 10.0 + weight * permittivity
    chosen_field = forward_field[mix_pairs[:, :, 0]]
    adjoint = adjoint_source / scale
    for sweep in range(ITERS):
        chosen_adjoint = adjoint[mix_pairs[:, :, 1]]
        kerr = complex_pairs(chosen_field, chosen_adjoint)
        turned = jnp.stack([-adjoint[:, 1], adjoint[:, 0]], axis=1)
        applied = plain_curl(adjoint) - weight * (permittivity * adjoint + sigma * turned + kerr_coef * mask * kerr)
        adjoint = adjoint + (adjoint_source - applied) / scale
    product = adjoint[:, 0] * forward_field[:, 0] - adjoint[:, 1] * forward_field[:, 1]
    gradient = mask * jnp.sum(squared[:, None, None, None, None] * product, axis=(0, 1))
    return adjoint, gradient
```

```python
import functools

import jax
import jax.numpy as jnp
from jax import lax
from jax.experimental import pallas as pl
from jax.experimental.pallas import tpu as pltpu
from jax.sharding import PartitionSpec as P

ITERS = 3
TILE = 4
DEEP = ITERS
NEAR = ITERS - 1

kerr_coef = 4.0
sigma_peak = 8.0

VMEM = pl.BlockSpec(memory_space=pltpu.VMEM)
SMEM = pl.BlockSpec(memory_space=pltpu.SMEM)


def round_up(value, unit):
    return (value + unit - 1) // unit * unit


def tile_mask(tiles_ref, plane, rows, lanes):
    place = lax.broadcasted_iota(jnp.int32, (rows, lanes), 0) // TILE
    mask = jnp.zeros((rows, lanes), jnp.float32)
    for col in range(rows // TILE):
        cell = tiles_ref[plane // TILE, col].astype(jnp.float32)
        mask = jnp.where(place == col, cell, mask)
    return mask


class Sizes:
    def __init__(self, owned, cells, counts):
        self.owned = owned
        self.values = owned * 6
        self.cx, self.cy, self.cz = cells
        self.gx, self.gy, self.ha = counts
        self.y_rows = round_up(self.cx * (self.values * (DEEP + NEAR) + DEEP), 8)
        self.d_rows = round_up(self.values * (DEEP**2 + NEAR**2) + DEEP**2, 8)
        self.x_tiles = self.values * (DEEP + NEAR) + DEEP


def edge_planes(cx, upper, depth):
    return list(range(cx - depth, cx)) if upper else list(range(depth))


def pack_kernel(sz, src_ref, fwd_ref, eps_ref, tiles_ref, *out_refs):
    pair = sz.gy == 2
    low_y = lax.axis_index("gy") == 0
    masks = [kerr_coef * tile_mask(tiles_ref, x, sz.cy, sz.cz) for x in range(sz.cx)]
    kinds = [(h, r, c) for h in range(sz.owned) for r in range(2) for c in range(3)]

    def x_face(ref, upper):
        at = 0
        for h, r, c in kinds:
            for x in edge_planes(sz.cx, upper, DEEP):
                ref[at] = src_ref[h, r, c, x]
                at += 1
        for h, r, c in kinds:
            for x in edge_planes(sz.cx, upper, NEAR):
                ref[at] = fwd_ref[h, r, c, x] * masks[x]
                at += 1
        for x in edge_planes(sz.cx, upper, DEEP):
            ref[at] = eps_ref[x]
            at += 1

    def rows_of(tile, top, depth):
        return tile[sz.cy - depth :] if top else tile[:depth]

    def y_part(planes_deep, planes_near, top):
        for h, r, c in kinds:
            for x in planes_deep:
                yield rows_of(src_ref[h, r, c, x], top, DEEP)
        for h, r, c in kinds:
            for x in planes_near:
                yield rows_of(fwd_ref[h, r, c, x] * masks[x], top, NEAR)
        for x in planes_deep:
            yield rows_of(eps_ref[x], top, DEEP)

    def write(ref, parts, others=None, choose=None):
        at = 0
        for part in parts:
            if others is not None:
                part = jnp.where(choose, part, next(others))
            ref[at : at + part.shape[0]] = part
            at += part.shape[0]
        if at < ref.shape[0]:
            ref[at:] = jnp.zeros((ref.shape[0] - at, sz.cz), jnp.float32)

    everywhere = list(range(sz.cx))

    def corner(upper, top):
        return y_part(edge_planes(sz.cx, upper, DEEP), edge_planes(sz.cx, upper, NEAR), top)

    x_face(out_refs[0], True)
    x_face(out_refs[1], False)
    if pair:
        write(
            out_refs[2],
            y_part(everywhere, everywhere, True),
            y_part(everywhere, everywhere, False),
            low_y,
        )
        write(out_refs[3], corner(False, True), corner(True, False), low_y)
        write(out_refs[4], corner(True, True), corner(False, False), low_y)
    else:
        write(out_refs[2], y_part(everywhere, everywhere, True))
        write(out_refs[3], y_part(everywhere, everywhere, False))
        write(out_refs[4], corner(True, False))
        write(out_refs[5], corner(False, True))
        write(out_refs[6], corner(True, True))
        write(out_refs[7], corner(False, False))


def sweep_kernel(
    sz, mix_ref, freq_ref, pml_ref, tiles_ref, eps_ref, *refs
):
    cx, cy, cz = sz.cx, sz.cy, sz.cz
    rows = cy + 8
    wide = cx + 2 * DEEP
    harmonics = sz.owned * sz.ha
    per_core = 10
    sides = [refs[per_core * s : per_core * (s + 1)] for s in range(sz.ha)]
    out_ref, grad_ref = refs[per_core * sz.ha : per_core * sz.ha + 2]
    base, first, second, fwd, invs, mags, eps_all = refs[per_core * sz.ha + 2 :]

    at_x, at_y, at_h = lax.axis_index("gx"), lax.axis_index("gy"), lax.axis_index("ha")
    pair = sz.gy == 2
    start = at_h * sz.owned

    def from_own(index):
        return lax.rem(index - start + harmonics, harmonics)

    def globally(position):
        return lax.rem(position + start, harmonics)

    squared = [freq_ref[globally(h)] * freq_ref[globally(h)] for h in range(harmonics)]

    sub = lax.broadcasted_iota(jnp.int32, (rows, cz), 0)
    lane = lax.broadcasted_iota(jnp.int32, (rows, cz), 1)
    row = jnp.where(sub < cy + 4, sub, sub - rows)
    place_y = row + at_y * cy
    keep_y = jnp.where((place_y >= 0) & (place_y < cy * sz.gy), 1.0, 0.0)

    def profile(width, place, count):
        reach = jnp.maximum(jnp.maximum(width - place, place - (count - 1 - width)), 0)
        return (reach.astype(jnp.float32) / jnp.full(reach.shape, width).astype(jnp.float32)) ** 2

    sigma_y = profile(pml_ref[1], place_y, cy * sz.gy)
    sigma_z = profile(pml_ref[2], lane, cz)

    def sigma_at(x):
        place = jnp.full((rows, cz), x - DEEP + at_x * cx)
        return sigma_peak * (profile(pml_ref[0], place, cx * sz.gx) + sigma_y + sigma_z)

    def keep_at(x):
        place = x - DEEP + at_x * cx
        inside = jnp.where((place >= 0) & (place < cx * sz.gx), 1.0, 0.0)
        return keep_y * inside

    def gate(value, low):
        if not pair:
            return value
        return jnp.where((at_y == 0) != low, value, 0.0)

    def halo(high, low):
        depth = high.shape[0]
        gap = jnp.zeros((8 - 2 * depth, cz), jnp.float32)
        return jnp.concatenate([gate(high, False), gap, gate(low, True)], axis=0)

    kinds = [(h, r, c) for h in range(sz.owned) for r in range(2) for c in range(3)]

    def x_index(field, kind, plane):
        n = kinds.index(kind)
        if field == 0:
            return n * DEEP + plane
        return sz.values * DEEP + n * NEAR + plane

    def y_rows_at(field, kind, plane, planes_deep, planes_near):
        n = kinds.index(kind)
        if field == 0:
            return (n * planes_deep + plane) * DEEP
        return sz.values * planes_deep * DEEP + (n * planes_near + plane) * NEAR

    def eps_rows_at(plane, planes_deep, planes_near):
        return sz.values * (planes_deep * DEEP + planes_near * NEAR) + plane * DEEP

    def take(ref, at, depth):
        return ref[at : at + depth]

    _, _, x_lo, x_hi, y_hi, y_lo, c_lo_hi, c_lo_lo, c_hi_hi, c_hi_lo = sides[0]
    tail = sz.values * (DEEP + NEAR)
    for d in range(DEEP):
        at = eps_rows_at(d, DEEP, NEAR)
        eps_all[d, :cy] = x_lo[tail + d]
        eps_all[d, cy:] = halo(take(c_lo_hi, at, DEEP), take(c_lo_lo, at, DEEP))
        eps_all[DEEP + cx + d, :cy] = x_hi[tail + d]
        eps_all[DEEP + cx + d, cy:] = halo(take(c_hi_hi, at, DEEP), take(c_hi_lo, at, DEEP))
    for x in range(cx):
        at = eps_rows_at(x, cx, cx)
        eps_all[DEEP + x, :cy] = eps_ref[x]
        eps_all[DEEP + x, cy:] = halo(take(y_hi, at, DEEP), take(y_lo, at, DEEP))

    def scales(x, _):
        eps = eps_all[x]
        for h in range(harmonics):
            invs[h, x] = 1.0 / (10.0 + squared[h] * eps)
        return 0

    lax.fori_loop(0, wide, scales, 0)

    masks = [kerr_coef * tile_mask(tiles_ref, x, cy, cz) for x in range(cx)]
    for s, side in enumerate(sides):
        own_src, own_fwd, x_lo, x_hi, y_hi, y_lo, c_lo_hi, c_lo_lo, c_hi_hi, c_hi_lo = side
        for kind in kinds:
            h, r, c = kind
            g = s * sz.owned + h
            for d in range(DEEP):
                at = y_rows_at(0, kind, d, DEEP, NEAR)
                x = d
                base[g, r, c, x, :cy] = x_lo[x_index(0, kind, d)] * invs[g, x, :cy]
                base[g, r, c, x, cy:] = (
                    halo(take(c_lo_hi, at, DEEP), take(c_lo_lo, at, DEEP)) * invs[g, x, cy:]
                )
                x = DEEP + cx + d
                base[g, r, c, x, :cy] = x_hi[x_index(0, kind, d)] * invs[g, x, :cy]
                base[g, r, c, x, cy:] = (
                    halo(take(c_hi_hi, at, DEEP), take(c_hi_lo, at, DEEP)) * invs[g, x, cy:]
                )
            for d in range(NEAR):
                at = y_rows_at(1, kind, d, DEEP, NEAR)
                fwd[g, r, c, d, :cy] = x_lo[x_index(1, kind, d)]
                fwd[g, r, c, d, cy:] = halo(take(c_lo_hi, at, NEAR), take(c_lo_lo, at, NEAR))
                fwd[g, r, c, NEAR + cx + d, :cy] = x_hi[x_index(1, kind, d)]
                fwd[g, r, c, NEAR + cx + d, cy:] = halo(
                    take(c_hi_hi, at, NEAR), take(c_hi_lo, at, NEAR)
                )
            for x in range(cx):
                at = y_rows_at(0, kind, x, cx, cx)
                base[g, r, c, DEEP + x, :cy] = own_src[h, r, c, x] * invs[g, DEEP + x, :cy]
                base[g, r, c, DEEP + x, cy:] = (
                    halo(take(y_hi, at, DEEP), take(y_lo, at, DEEP)) * invs[g, DEEP + x, cy:]
                )
                at = y_rows_at(1, kind, x, cx, cx)
                fwd[g, r, c, NEAR + x, :cy] = own_fwd[h, r, c, x] * masks[x]
                fwd[g, r, c, NEAR + x, cy:] = halo(take(y_hi, at, NEAR), take(y_lo, at, NEAR))

    def y_ahead(v):
        return pltpu.roll(v, rows - 1, 0)

    def y_behind(v):
        return pltpu.roll(v, 1, 0)

    def z_ahead(v):
        return jnp.where(lane == cz - 1, 0.0, pltpu.roll(v, cz - 1, 1))

    def z_behind(v):
        return jnp.where(lane == 0, 0.0, pltpu.roll(v, 1, 1))

    def forward_mags(v_ref, h, r, x, keep):
        fx, fy, fz = v_ref[h, r, 0, x], v_ref[h, r, 1, x], v_ref[h, r, 2, x]
        next_y, next_z = v_ref[h, r, 1, x + 1], v_ref[h, r, 2, x + 1]
        mag_y = ((z_ahead(fx) - fx) - (next_z - fz)) * keep
        mag_z = ((next_y - fy) - (y_ahead(fx) - fx)) * keep
        return fx, fy, fz, mag_y, mag_z

    pairs = [
        (from_own(mix_ref[globally(h), p, 0]), from_own(mix_ref[globally(h), p, 1]))
        for h in range(harmonics)
        for p in range(mix_ref.shape[1])
    ]
    count = mix_ref.shape[1]

    def sweep(k, v_ref, store):
        lo, hi = k + 1, wide - 1 - k

        keep = keep_at(k)
        for h in range(harmonics):
            for r in range(2):
                _, _, _, mag_y, mag_z = forward_mags(v_ref, h, r, k, keep)
                mags[h, r, 0] = mag_y
                mags[h, r, 1] = mag_z

        def body(x, _):
            keep = keep_at(x)
            sigma = sigma_at(x)
            results = []
            for h in range(harmonics):
                inv = invs[h, x]
                slope = 2.0 - 10.0 * inv
                absorb = squared[h] * sigma
                curls = []
                here = []
                for r in range(2):
                    fx, fy, fz, mag_y, mag_z = forward_mags(v_ref, h, r, x, keep)
                    mag_x = ((y_ahead(fz) - fz) - (z_ahead(fy) - fy)) * keep
                    past_y, past_z = mags[h, r, 0], mags[h, r, 1]
                    mags[h, r, 0] = mag_y
                    mags[h, r, 1] = mag_z
                    curls.append(
                        (
                            (mag_z - y_behind(mag_z)) - (mag_y - z_behind(mag_y)),
                            (mag_x - z_behind(mag_x)) - (mag_z - past_z),
                            (mag_y - past_y) - (mag_x - y_behind(mag_x)),
                        )
                    )
                    here.append((fx, fy, fz))
                for c in range(3):
                    real = imag = None
                    for p in range(count):
                        a, b = pairs[h * count + p]
                        fr, fi = fwd[a, 0, c, x - 1], fwd[a, 1, c, x - 1]
                        vr, vi = v_ref[b, 0, c, x], v_ref[b, 1, c, x]
                        one = fr * vr - fi * vi
                        two = fr * vi + fi * vr
                        real = one if real is None else real + one
                        imag = two if imag is None else imag + two
                    vr, vi = here[0][c], here[1][c]
                    new_r = (
                        base[h, 0, c, x]
                        + vr * slope
                        + inv * (squared[h] * real - absorb * vi - curls[0][c])
                    )
                    new_i = (
                        base[h, 1, c, x]
                        + vi * slope
                        + inv * (squared[h] * imag + absorb * vr - curls[1][c])
                    )
                    results.append((h, c, new_r, new_i))
                store(x, keep, results)
                results = []
            return 0

        lax.fori_loop(lo, hi, body, 0)

    def store_in(ref):
        def store(x, keep, results):
            for h, c, new_r, new_i in results:
                ref[h, 0, c, x] = new_r * keep
                ref[h, 1, c, x] = new_i * keep

        return store

    def store_out(x, keep, results):
        for h, c, new_r, new_i in results:
            new_r, new_i = new_r[:cy], new_i[:cy]
            if h < sz.owned:
                out_ref[h, 0, c, x - DEEP] = new_r
                out_ref[h, 1, c, x - DEEP] = new_i
            term = (squared[h] / kerr_coef) * (
                new_r * fwd[h, 0, c, x - 1, :cy] - new_i * fwd[h, 1, c, x - 1, :cy]
            )
            if h == 0 and c == 0:
                grad_ref[x - DEEP] = term
            else:
                grad_ref[x - DEEP] += term

    sweep(0, base, store_in(first))
    sweep(1, first, store_in(second))
    sweep(2, second, store_out)


def chain(count_x, count_y, step_x, step_y):
    sends = []
    for x in range(count_x):
        for y in range(count_y):
            to_x, to_y = x + step_x, y + step_y
            if 0 <= to_x < count_x and 0 <= to_y < count_y:
                sends.append((x * count_y + y, to_x * count_y + to_y))
    return sends


def shards(
    forward_field, adjoint_source, permittivity, frequency, design_tiles, mix_pairs, pml_width
):
    counts = tuple(lax.axis_size(name) for name in ("gx", "gy", "ha"))
    sz = Sizes(forward_field.shape[0], permittivity.shape, counts)
    pair = sz.gy == 2
    f32 = jnp.float32
    x_buf = jax.ShapeDtypeStruct((sz.x_tiles, sz.cy, sz.cz), f32)
    y_buf = jax.ShapeDtypeStruct((sz.y_rows, sz.cz), f32)
    d_buf = jax.ShapeDtypeStruct((sz.d_rows, sz.cz), f32)
    n_y, n_d = (1, 2) if pair else (2, 4)
    packed = pl.pallas_call(
        functools.partial(pack_kernel, sz),
        out_shape=[x_buf, x_buf] + [y_buf] * n_y + [d_buf] * n_d,
        in_specs=[VMEM, VMEM, VMEM, SMEM],
        out_specs=[VMEM] * (2 + n_y + n_d),
        name="pack",
    )(adjoint_source, forward_field, permittivity, design_tiles)

    def send(buffer, *steps):
        pairs = [edge for step in steps for edge in chain(sz.gx, sz.gy, *step)]
        return lax.ppermute(buffer, ("gx", "gy"), pairs)

    x_lo = send(packed[0], (1, 0))
    x_hi = send(packed[1], (-1, 0))
    if pair:
        y_any = send(packed[2], (0, 1), (0, -1))
        anti = send(packed[3], (-1, 1), (1, -1))
        main = send(packed[4], (1, 1), (-1, -1))
        got = [x_lo, x_hi, y_any, anti, main]
        order = (0, 1, 2, 2, 3, 4, 4, 3)
    else:
        got = [
            x_lo,
            x_hi,
            send(packed[3], (0, -1)),
            send(packed[2], (0, 1)),
            send(packed[4], (1, -1)),
            send(packed[6], (1, 1)),
            send(packed[7], (-1, -1)),
            send(packed[5], (-1, 1)),
        ]
        order = (0, 1, 2, 3, 4, 5, 6, 7)

    own = [adjoint_source, forward_field] + got
    flip = [(i, sz.ha - 1 - i) for i in range(sz.ha)]
    other = [lax.ppermute(buffer, "ha", flip) for buffer in own]

    def spread(buffers):
        return buffers[:2] + [buffers[2 + i] for i in order]

    rows, wide, harmonics = sz.cy + 8, sz.cx + 2 * DEEP, sz.owned * sz.ha
    field = (harmonics, 2, 3, wide, rows, sz.cz)
    near = (harmonics, 2, 3, wide - 2, rows, sz.cz)
    adjoint, gradient = pl.pallas_call(
        functools.partial(sweep_kernel, sz),
        out_shape=[
            jax.ShapeDtypeStruct(adjoint_source.shape, f32),
            jax.ShapeDtypeStruct(permittivity.shape, f32),
        ],
        in_specs=[SMEM] * 4 + [VMEM] * 21,
        out_specs=[VMEM, VMEM],
        scratch_shapes=[
            pltpu.VMEM(field, f32),
            pltpu.VMEM(field, f32),
            pltpu.VMEM(field, f32),
            pltpu.VMEM(near, f32),
            pltpu.VMEM((harmonics, wide, rows, sz.cz), f32),
            pltpu.VMEM((harmonics, 2, 2, rows, sz.cz), f32),
            pltpu.VMEM((wide, rows, sz.cz), f32),
        ],
        compiler_params=pltpu.CompilerParams(vmem_limit_bytes=48 * 1024 * 1024),
        name="sweeps",
    )(
        mix_pairs,
        frequency,
        pml_width,
        design_tiles,
        permittivity,
        *spread(own),
        *spread(other),
    )
    return (adjoint, gradient)


def solution(mesh):
    return jax.shard_map(
        shards,
        mesh=mesh,
        in_specs=(
            P("ha", None, None, ("cand", "gx"), "gy", None),
            P("ha", None, None, ("cand", "gx"), "gy", None),
            P(("cand", "gx"), "gy", None),
            P(),
            P(("cand", "gx"), "gy"),
            P(),
            P(),
        ),
        out_specs=(P("ha", None, None, ("cand", "gx"), "gy", None), P(("cand", "gx"), "gy", None)),
        check_vma=False,
    )
```

```python
import functools

import jax
import jax.numpy as jnp
from jax import lax
from jax.experimental import pallas as pl
from jax.experimental.pallas import tpu as pltpu
from jax.sharding import PartitionSpec as P

ITERS = 3
TILE = 4
DEEP = ITERS
NEAR = ITERS - 1
LANES = 128
SUBS = 8

kerr_coef = 4.0
sigma_peak = 8.0

VMEM = pl.BlockSpec(memory_space=pltpu.VMEM)
SMEM = pl.BlockSpec(memory_space=pltpu.SMEM)
ANY = pl.BlockSpec(memory_space=pl.ANY)


class Sizes:
    def __init__(self, owned, cells, counts):
        self.owned = owned
        self.cx, self.cy, self.cz = cells
        self.gx, self.gy, self.ha = counts
        self.harmonics = owned * self.ha
        self.halves = self.cz // LANES
        self.wide = self.cx + 2 * DEEP
        self.rows = self.cy + 2 * DEEP + 2
        self.kinds = [(h, r, c) for h in range(owned) for r in range(2) for c in range(3)]
        self.colours = (0,) if self.gy == 2 else (0, 1)
        self.x_tiles = len(self.kinds) * (DEEP + NEAR) + DEEP
        whole = [(x, DEEP) for x in range(self.cx)]
        self.side = self.groups(whole, [(x, NEAR) for x in range(self.cx)])
        anti = [(d, DEEP) for d in range(DEEP)]
        self.anti = self.groups(anti, [(d, NEAR) for d in range(NEAR)])
        main = [(d, DEEP - 1 - d) for d in range(DEEP - 1)]
        self.main = self.groups(main, [(d, NEAR - 1 - d) for d in range(NEAR - 1)])

    def groups(self, deep, near):
        listed, at = [], SUBS
        for field, planes in ((0, deep), (1, near)):
            for kind in self.kinds:
                for plane, depth in planes:
                    listed.append((field, kind, plane, depth, at))
                    at += depth
        for plane, depth in deep:
            listed.append((2, None, plane, depth, at))
            at += depth
        return listed

    def length(self, groups):
        last = groups[-1]
        return (last[4] + SUBS + SUBS - 1) // SUBS * SUBS


def half(z):
    return slice(z * LANES, (z + 1) * LANES)


def tile_mask(tiles_ref, plane, rows):
    place = lax.broadcasted_iota(jnp.int32, (rows, LANES), 0) // TILE
    mask = jnp.zeros((rows, LANES), jnp.float32)
    for col in range(rows // TILE):
        cell = tiles_ref[plane // TILE, col].astype(jnp.float32)
        mask = jnp.where(place == col, cell, mask)
    return mask


def plane_mask(tiles_ref, plane, sz):
    mask = tile_mask(tiles_ref, 0, sz.cy)
    for x in range(TILE, sz.cx, TILE):
        mask = jnp.where(plane >= x, tile_mask(tiles_ref, x, sz.cy), mask)
    return kerr_coef * mask


def x_is_high(colour):
    return lax.rem(lax.axis_index("gx") + colour, 2) == 0


def y_is_high(colour):
    return lax.rem(lax.axis_index("gy") + colour, 2) == 0


def pack_x_kernel(sz, src_ref, fwd_ref, eps_ref, tiles_ref, even_ref, odd_ref):
    for colour, ref in ((0, even_ref), (1, odd_ref)):
        high = x_is_high(colour)
        deep = jnp.where(high, sz.cx - DEEP, 0)
        near = jnp.where(high, sz.cx - NEAR, 0)
        at = 0
        for h, r, c in sz.kinds:
            for d in range(DEEP):
                ref[at] = src_ref[h, r, c, deep + d]
                at += 1
        masks = [plane_mask(tiles_ref, near + d, sz) for d in range(NEAR)]
        for h, r, c in sz.kinds:
            for d in range(NEAR):
                for z in range(sz.halves):
                    ref[at, :, half(z)] = fwd_ref[h, r, c, near + d, :, half(z)] * masks[d]
                at += 1
        for d in range(DEEP):
            ref[at] = eps_ref[deep + d]
            at += 1


def pack_y_kernel(sz, src_ref, fwd_ref, eps_ref, tiles_ref, *out_refs):
    outs = iter(out_refs)

    def fill(ref, groups, top, plane_of):
        for field, kind, plane, depth, at in reversed(groups):
            x = plane_of(plane)
            shift = sz.cy - depth
            for z in range(sz.halves):
                if field == 2:
                    tile = eps_ref[x, :, half(z)]
                elif field == 0:
                    tile = src_ref[(*kind, x, slice(None), half(z))]
                else:
                    tile = fwd_ref[(*kind, x, slice(None), half(z))] * plane_mask(tiles_ref, x, sz)
                tile = jnp.where(top, tile, pltpu.roll(tile, shift, 0))
                ref[z, at - shift : at + depth] = tile

    for colour in sz.colours:
        top = y_is_high(colour)
        fill(next(outs), sz.side, top, lambda plane: plane)
        for groups, upper in ((sz.anti, jnp.logical_not(top)), (sz.main, top)):
            fill(
                next(outs),
                groups,
                top,
                lambda plane, upper=upper: jnp.where(upper, sz.cx - 1 - plane, plane),
            )


def sweep_kernel(sz, mix_hbm, freq_hbm, pml_hbm, tiles_hbm, eps_hbm, *refs):
    cx, cy, cz, halves = sz.cx, sz.cy, sz.cz, sz.halves
    wide, harmonics = sz.wide, sz.harmonics
    per_core = 4 + 3 * len(sz.colours)
    sides = [refs[per_core * s : per_core * (s + 1)] for s in range(sz.ha)]
    out_ref, grad_ref = refs[per_core * sz.ha : per_core * sz.ha + 2]
    scratch = refs[per_core * sz.ha + 2 :]
    base, first, second, fwd, invs, mags, eps_all = scratch[:7]
    mix_ref, freq_ref, pml_ref, tiles_ref, eps_ref, sems = scratch[7:]

    copies = [
        pltpu.make_async_copy(source, target, sems.at[i])
        for i, (source, target) in enumerate(
            (
                (mix_hbm, mix_ref),
                (freq_hbm, freq_ref),
                (pml_hbm, pml_ref),
                (tiles_hbm, tiles_ref),
                (eps_hbm, eps_ref),
            )
        )
    ]
    for copy in copies:
        copy.start()

    at_x, at_y, at_h = lax.axis_index("gx"), lax.axis_index("gy"), lax.axis_index("ha")
    start = at_h * sz.owned

    def from_own(index):
        return lax.rem(index - start + harmonics, harmonics)

    def globally(position):
        return lax.rem(position + start, harmonics)

    nothing = jnp.zeros((DEEP, LANES), jnp.float32)
    for g in range(harmonics):
        for r in range(2):
            for z in range(halves):
                for c in range(3):
                    for x in range(wide):
                        base[g, r, c, x, z, :DEEP] = nothing
                        base[g, r, c, x, z, DEEP + cy : DEEP + cy + DEEP] = nothing
                    for x in range(wide - 2):
                        fwd[g, r, c, x, z, :DEEP] = nothing
                        fwd[g, r, c, x, z, DEEP + cy : DEEP + cy + DEEP] = nothing
    for x in range(wide):
        for z in range(halves):
            eps_all[x, z] = jnp.zeros((sz.rows, LANES), jnp.float32)

    for copy in copies:
        copy.wait()

    squared = [freq_ref[globally(h)] * freq_ref[globally(h)] for h in range(harmonics)]
    lane = lax.broadcasted_iota(jnp.int32, (SUBS, LANES), 1)
    sub = lax.broadcasted_iota(jnp.int32, (SUBS, LANES), 0)

    def x_start(colour, depth):
        return jnp.where(x_is_high(colour), DEEP + cx, DEEP - depth)

    def y_spots(colour, corner=None):
        high_y = y_is_high(colour)
        if corner is None:
            plane_of = lambda plane: DEEP + plane
        else:
            high_x = jnp.logical_not(high_y) if corner == "anti" else high_y
            plane_of = lambda plane: jnp.where(high_x, DEEP + cx + plane, DEEP - 1 - plane)
        row_of = lambda depth: jnp.where(high_y, DEEP + cy, DEEP - depth)
        return plane_of, row_of

    def row_buffers(side):
        buffers = side[4:]
        for i, colour in enumerate(sz.colours):
            yield buffers[3 * i], sz.side, y_spots(colour)
            yield buffers[3 * i + 1], sz.anti, y_spots(colour, "anti")
            yield buffers[3 * i + 2], sz.main, y_spots(colour, "main")

    count = len(sz.kinds)
    for colour in (0, 1):
        buffer, x0 = sides[0][2 + colour], x_start(colour, DEEP)
        for d in range(DEEP):
            for z in range(halves):
                eps_all[x0 + d, z, DEEP : DEEP + cy] = buffer[count * (DEEP + NEAR) + d, :, half(z)]
    for x in range(cx):
        for z in range(halves):
            eps_all[DEEP + x, z, DEEP : DEEP + cy] = eps_ref[x, :, half(z)]
    for buffer, groups, (plane_of, row_of) in row_buffers(sides[0]):
        for field, kind, plane, depth, at in groups:
            if field == 2:
                for z in range(halves):
                    eps_all[plane_of(plane), z, pl.ds(row_of(depth), depth)] = buffer[
                        z, at : at + depth
                    ]

    def keep_rows(row):
        place = sub + (row - DEEP) + at_y * cy
        return (place >= 0) & (place < cy * sz.gy)

    def keep_plane(x):
        place = x - DEEP + at_x * cx
        return (place >= 0) & (place < cx * sz.gx)

    def scales(x, _):
        inside = jnp.where(keep_plane(x), 1.0, 0.0)
        for row in (0, SUBS):
            keep = jnp.where(keep_rows(row), inside, 0.0)
            for z in range(halves):
                eps = eps_all[x, z, row : row + SUBS]
                for h in range(harmonics):
                    invs[h, x, z, row : row + SUBS] = keep / (10.0 + squared[h] * eps)
        return 0

    lax.fori_loop(0, wide, scales, 0)

    masks = [kerr_coef * tile_mask(tiles_ref, x, cy) for x in range(cx)]
    inner = slice(DEEP, DEEP + cy)
    for s, side in enumerate(sides):
        own_src, own_fwd = side[:2]
        for n, kind in enumerate(sz.kinds):
            h, r, c = kind
            g = s * sz.owned + h
            for z in range(halves):
                for x in range(cx):
                    base[g, r, c, DEEP + x, z, inner] = (
                        own_src[h, r, c, x, :, half(z)] * invs[g, DEEP + x, z, inner]
                    )
                    fwd[g, r, c, NEAR + x, z, inner] = own_fwd[h, r, c, x, :, half(z)] * masks[x]
                for colour in (0, 1):
                    buffer = side[2 + colour]
                    x0, x1 = x_start(colour, DEEP), x_start(colour, NEAR) - 1
                    for d in range(DEEP):
                        base[g, r, c, x0 + d, z, inner] = (
                            buffer[n * DEEP + d, :, half(z)] * invs[g, x0 + d, z, inner]
                        )
                    for d in range(NEAR):
                        fwd[g, r, c, x1 + d, z, inner] = buffer[
                            count * DEEP + n * NEAR + d, :, half(z)
                        ]
        for buffer, groups, (plane_of, row_of) in row_buffers(side):
            for field, kind, plane, depth, at in groups:
                if field == 2:
                    continue
                h, r, c = kind
                g = s * sz.owned + h
                x, rows = plane_of(plane), pl.ds(row_of(depth), depth)
                for z in range(halves):
                    got = buffer[z, at : at + depth]
                    if field == 0:
                        base[g, r, c, x, z, rows] = got * invs[g, x, z, rows]
                    else:
                        fwd[g, r, c, x - 1, z, rows] = got

    def profile(width, place, cells):
        reach = jnp.maximum(jnp.maximum(width - place, place - (cells - 1 - width)), 0)
        return (reach.astype(jnp.float32) / jnp.full(reach.shape, width).astype(jnp.float32)) ** 2

    sigma_z = [profile(pml_ref[2], lane + z * LANES, cz) for z in range(halves)]

    def z_ahead(parts):
        turned = [pltpu.roll(v, LANES - 1, 1) for v in parts]
        following = turned[1:] + [0.0]
        return [jnp.where(lane == LANES - 1, f, t) for t, f in zip(turned, following)]

    def z_behind(parts):
        turned = [pltpu.roll(v, 1, 1) for v in parts]
        previous = [0.0] + turned[:-1]
        return [jnp.where(lane == 0, p, t) for t, p in zip(turned, previous)]

    pairs = [
        (from_own(mix_ref[p, 0, globally(h)]), from_own(mix_ref[p, 1, globally(h)]))
        for h in range(harmonics)
        for p in range(mix_ref.shape[0])
    ]
    mixes = mix_ref.shape[0]
    zs = range(halves)

    def sweep(k, v_ref, store):
        lo, hi = k + 1, wide - 1 - k
        top = DEEP + cy + NEAR - k
        out_rows = sorted({k + 1, top - SUBS})
        mag_rows = sorted({k, top - SUBS})
        sigma_y = {
            row: profile(pml_ref[1], sub + (row - DEEP) + at_y * cy, cy * sz.gy) for row in out_rows
        }

        def write_mags(x, comps):
            slot = lax.rem(x, 2)
            inside = x - DEEP + at_x * cx >= 0
            for row in mag_rows:
                mask = (sub + (row - DEEP) + at_y * cy >= 0) & inside
                for g in range(harmonics):
                    for r in range(2):
                        here = [
                            [v_ref[g, r, c, x, z, row : row + SUBS] for z in zs] for c in range(3)
                        ]
                        next_y, next_z = [
                            [v_ref[g, r, c, x + 1, z, row : row + SUBS] for z in zs] for c in (1, 2)
                        ]
                        above_x, above_z = [
                            [v_ref[g, r, c, x, z, row + 1 : row + 1 + SUBS] for z in zs]
                            for c in (0, 2)
                        ]
                        fx, fy, fz = here
                        after_x = z_ahead(fx)
                        found = {}
                        if 0 in comps:
                            after_y = z_ahead(fy)
                            found[0] = [
                                (above_z[z] - fz[z]) - (after_y[z] - fy[z]) for z in zs
                            ]
                        found[1] = [(after_x[z] - fx[z]) - (next_z[z] - fz[z]) for z in zs]
                        found[2] = [(next_y[z] - fy[z]) - (above_x[z] - fx[z]) for z in zs]
                        for c, parts in found.items():
                            for z in zs:
                                pltpu.store(
                                    mags.at[slot, g, r, c, z, row : row + SUBS],
                                    parts[z],
                                    mask=mask,
                                )

        for slot in range(2):
            for g in range(harmonics):
                for r in range(2):
                    for c in range(3):
                        for z in zs:
                            mags[slot, g, r, c, z] = jnp.zeros((sz.rows, LANES), jnp.float32)
        write_mags(k, (1, 2))

        def body(x, _):
            write_mags(x, (0, 1, 2))
            slot, past = lax.rem(x, 2), lax.rem(x + 1, 2)
            twice = jnp.where(keep_plane(x), 2.0, 0.0)
            place = jnp.full((SUBS, LANES), x - DEEP + at_x * cx)
            sigma_x = profile(pml_ref[0], place, cx * sz.gx)
            for row in out_rows:
                span, below = slice(row, row + SUBS), slice(row - 1, row - 1 + SUBS)
                double = jnp.where(keep_rows(row), twice, 0.0)
                sigma = [sigma_peak * (sigma_x + sigma_y[row] + sigma_z[z]) for z in zs]
                for h in range(harmonics):
                    curls = []
                    for r in range(2):
                        mag = [[mags[slot, h, r, c, z, span] for z in zs] for c in range(3)]
                        low_x, low_z = [
                            [mags[slot, h, r, c, z, below] for z in zs] for c in (0, 2)
                        ]
                        past_y, past_z = [
                            [mags[past, h, r, c, z, span] for z in zs] for c in (1, 2)
                        ]
                        before_x, before_y = z_behind(mag[0]), z_behind(mag[1])
                        curls.append(
                            [
                                [
                                    (mag[2][z] - low_z[z]) - (mag[1][z] - before_y[z]),
                                    (mag[0][z] - before_x[z]) - (mag[2][z] - past_z[z]),
                                    (mag[1][z] - past_y[z]) - (mag[0][z] - low_x[z]),
                                ]
                                for z in zs
                            ]
                        )
                    for z in zs:
                        inv = invs[h, x, z, span]
                        slope = double - 10.0 * inv
                        absorb = squared[h] * sigma[z]
                        for c in range(3):
                            real = imag = None
                            for p in range(mixes):
                                a, b = pairs[h * mixes + p]
                                fr, fi = [fwd[a, r, c, x - 1, z, span] for r in range(2)]
                                vr, vi = [v_ref[b, r, c, x, z, span] for r in range(2)]
                                one, two = fr * vr - fi * vi, fr * vi + fi * vr
                                real = one if real is None else real + one
                                imag = two if imag is None else imag + two
                            vr, vi = [v_ref[h, r, c, x, z, span] for r in range(2)]
                            new_r = (
                                base[h, 0, c, x, z, span]
                                + vr * slope
                                + inv * (squared[h] * real - absorb * vi - curls[0][z][c])
                            )
                            new_i = (
                                base[h, 1, c, x, z, span]
                                + vi * slope
                                + inv * (squared[h] * imag + absorb * vr - curls[1][z][c])
                            )
                            store(h, c, x, z, span, new_r, new_i)
            return 0

        lax.fori_loop(lo, hi, body, 0)

    def store_in(ref):
        def store(h, c, x, z, span, new_r, new_i):
            ref[h, 0, c, x, z, span] = new_r
            ref[h, 1, c, x, z, span] = new_i

        return store

    sums = {}

    def store_out(h, c, x, z, span, new_r, new_i):
        if h < sz.owned:
            out_ref[h, 0, c, x - DEEP, :, half(z)] = new_r
            out_ref[h, 1, c, x - DEEP, :, half(z)] = new_i
        term = (squared[h] / kerr_coef) * (
            new_r * fwd[h, 0, c, x - 1, z, span] - new_i * fwd[h, 1, c, x - 1, z, span]
        )
        if h == 0 and c == 0:
            sums[z] = term
        else:
            sums[z] = sums[z] + term
        if h == harmonics - 1 and c == 2:
            grad_ref[x - DEEP, :, half(z)] = sums[z]

    sweep(0, base, store_in(first))
    sweep(1, first, store_in(second))
    sweep(2, second, store_out)


def swaps(count_x, count_y, partner):
    sends = []
    for x in range(count_x):
        for y in range(count_y):
            to_x, to_y = partner(x, y)
            if 0 <= to_x < count_x and 0 <= to_y < count_y:
                sends.append((x * count_y + y, to_x * count_y + to_y))
    return sends


def shards(
    forward_field, adjoint_source, permittivity, frequency, design_tiles, mix_pairs, pml_width
):
    counts = tuple(lax.axis_size(name) for name in ("gx", "gy", "ha"))
    sz = Sizes(forward_field.shape[0], permittivity.shape, counts)
    f32 = jnp.float32
    x_buf = jax.ShapeDtypeStruct((sz.x_tiles, sz.cy, sz.cz), f32)
    even, odd = pl.pallas_call(
        functools.partial(pack_x_kernel, sz),
        out_shape=[x_buf, x_buf],
        in_specs=[VMEM, VMEM, VMEM, SMEM],
        out_specs=[VMEM, VMEM],
        name="pack_x",
    )(adjoint_source, forward_field, permittivity, design_tiles)
    row_bufs = [
        jax.ShapeDtypeStruct((sz.halves, sz.length(groups), LANES), f32)
        for groups in (sz.side, sz.anti, sz.main)
    ] * len(sz.colours)
    packed = pl.pallas_call(
        functools.partial(pack_y_kernel, sz),
        out_shape=row_bufs,
        in_specs=[VMEM, VMEM, VMEM, SMEM],
        out_specs=[VMEM] * len(row_bufs),
        name="pack_y",
    )(adjoint_source, forward_field, permittivity, design_tiles)

    def send(buffer, partner):
        return lax.ppermute(buffer, ("gx", "gy"), swaps(sz.gx, sz.gy, partner))

    def step(place, colour):
        return 1 if (place + colour) % 2 == 0 else -1

    got = [
        send(even, lambda x, y: (x + step(x, 0), y)),
        send(odd, lambda x, y: (x + step(x, 1), y)),
    ]
    for i, colour in enumerate(sz.colours):
        got += [
            send(packed[3 * i], lambda x, y: (x, y + step(y, colour))),
            send(packed[3 * i + 1], lambda x, y: (x - step(y, colour), y + step(y, colour))),
            send(packed[3 * i + 2], lambda x, y: (x + step(y, colour), y + step(y, colour))),
        ]

    own = [adjoint_source, forward_field] + got
    flip = [(i, sz.ha - 1 - i) for i in range(sz.ha)]
    other = [lax.ppermute(buffer, "ha", flip) for buffer in own]

    def field(planes):
        return pltpu.VMEM((sz.harmonics, 2, 3, planes, sz.halves, sz.rows, LANES), f32)

    mix_by_pair = jnp.transpose(mix_pairs, (1, 2, 0))
    adjoint, gradient = pl.pallas_call(
        functools.partial(sweep_kernel, sz),
        out_shape=[
            jax.ShapeDtypeStruct(adjoint_source.shape, f32),
            jax.ShapeDtypeStruct(permittivity.shape, f32),
        ],
        in_specs=[ANY] * 5 + [VMEM] * (2 * len(own)),
        out_specs=[VMEM, VMEM],
        scratch_shapes=[
            field(sz.wide),
            field(sz.wide),
            field(sz.wide),
            field(sz.wide - 2),
            pltpu.VMEM((sz.harmonics, sz.wide, sz.halves, sz.rows, LANES), f32),
            pltpu.VMEM((2, sz.harmonics, 2, 3, sz.halves, sz.rows, LANES), f32),
            pltpu.VMEM((sz.wide, sz.halves, sz.rows, LANES), f32),
            pltpu.SMEM(mix_by_pair.shape, jnp.int32),
            pltpu.SMEM(frequency.shape, f32),
            pltpu.SMEM(pml_width.shape, jnp.int32),
            pltpu.SMEM(design_tiles.shape, jnp.int32),
            pltpu.VMEM(permittivity.shape, f32),
            pltpu.SemaphoreType.DMA((5,)),
        ],
        compiler_params=pltpu.CompilerParams(vmem_limit_bytes=32 * 1024 * 1024),
        name="sweeps",
    )(mix_by_pair, frequency, pml_width, design_tiles, permittivity, *own, *other)
    return (adjoint, gradient)


def solution(mesh):
    return jax.shard_map(
        shards,
        mesh=mesh,
        in_specs=(
            P("ha", None, None, ("cand", "gx"), "gy", None),
            P("ha", None, None, ("cand", "gx"), "gy", None),
            P(("cand", "gx"), "gy", None),
            P(),
            P(("cand", "gx"), "gy"),
            P(),
            P(),
        ),
        out_specs=(P("ha", None, None, ("cand", "gx"), "gy", None), P(("cand", "gx"), "gy", None)),
        check_vma=False,
    )
```

```python
import functools

import jax
import jax.numpy as jnp
from jax import lax
from jax.experimental import pallas as pl
from jax.experimental.pallas import tpu as pltpu
from jax.sharding import PartitionSpec as P


ITERS = 3
TILE = 4
DEEP = ITERS
NEAR = ITERS - 1
LANES = 128
SUBS = 8

kerr_coef = 4.0
sigma_peak = 8.0

VMEM = pl.BlockSpec(memory_space=pltpu.VMEM)
SMEM = pl.BlockSpec(memory_space=pltpu.SMEM)


class Sizes:
    def __init__(self, owned, cells, counts):
        self.owned = owned
        self.cx, self.cy, self.cz = cells
        self.gx, self.gy, self.ha = counts
        self.harmonics = owned * self.ha
        self.halves = self.cz // LANES
        self.wide = self.cx + 2 * DEEP
        self.rows = self.cy + 2 * DEEP + 2
        self.kinds = [(h, r, c) for h in range(owned) for r in range(2) for c in range(3)]
        self.colours = (0,) if self.gy == 2 else (0, 1)
        assert self.cy == SUBS and self.cx >= DEEP
        planes = range(self.cx)
        self.side, self.side_rows = self.groups(
            [(x, 0, DEEP) for x in planes], [(x, 0, NEAR) for x in planes]
        )
        self.main, at = self.groups(
            [(p, 0, DEEP - 1 - p) for p in range(DEEP - 1)],
            [(p, 0, NEAR - 1 - p) for p in range(NEAR - 1)],
        )
        rest, self.corner_rows = self.groups(
            [(p, DEEP - 1 - p, DEEP) for p in range(DEEP)],
            [(p, NEAR - 1 - p, NEAR) for p in range(NEAR)],
            at,
        )
        self.corner = self.main + rest
        self.main_rows = round_up(at)
        edges = len(self.colours) - 1
        self.far, self.far_rows = self.groups(
            [(p, DEEP, self.cy - edges * DEEP) for p in range(DEEP)],
            [(p, NEAR, self.cy - edges * NEAR) for p in range(NEAR)],
        )

    def groups(self, deep, near, at=SUBS):
        listed = []
        for field, kinds, planes in ((0, self.kinds, deep), (1, self.kinds, near), (2, [()], deep)):
            for kind in kinds:
                for plane, low, high in planes:
                    listed.append((field, kind, plane, low, high, at))
                    at += high - low
        return listed, at


def round_up(rows):
    return (rows + SUBS - 1) // SUBS * SUBS


def half(z):
    return slice(z * LANES, (z + 1) * LANES)


def tile_mask(tiles_ref, plane, rows):
    place = lax.broadcasted_iota(jnp.int32, (rows, LANES), 0) // TILE
    mask = jnp.zeros((rows, LANES), jnp.float32)
    for col in range(rows // TILE):
        cell = tiles_ref[plane // TILE, col].astype(jnp.float32)
        mask = jnp.where(place == col, cell, mask)
    return mask


def plane_mask(tiles_ref, plane, sz):
    mask = tile_mask(tiles_ref, 0, sz.cy)
    for x in range(TILE, sz.cx, TILE):
        mask = jnp.where(plane >= x, tile_mask(tiles_ref, x, sz.cy), mask)
    return kerr_coef * mask


def x_is_high(colour):
    return lax.rem(lax.axis_index("gx") + colour, 2) == 0


def y_is_high(colour):
    return lax.rem(lax.axis_index("gy") + colour, 2) == 0


def fill(sz, ref, groups, top, plane_of, inputs):
    src_ref, fwd_ref, eps_ref, tiles_ref = inputs
    mask = plane_mask(tiles_ref, 0, sz) if sz.cx <= TILE else None
    for field, kind, plane, low, high, at in reversed(groups):
        x = plane_of(plane)
        room = sz.cy - (high - low)
        for z in range(sz.halves):
            if field == 2:
                tile = eps_ref[x, :, half(z)]
            elif field == 0:
                tile = src_ref[(*kind, x, slice(None), half(z))]
            else:
                scale = plane_mask(tiles_ref, x, sz) if mask is None else mask
                tile = fwd_ref[(*kind, x, slice(None), half(z))] * scale
            if_top = pltpu.roll(tile, low, 0) if low else tile
            if_not = pltpu.roll(tile, sz.cy - high, 0) if high < sz.cy else tile
            ref[z, at - room : at + high - low] = jnp.where(top, if_top, if_not)


def from_face(sz, colour):
    upper = x_is_high(colour)
    return lambda plane: jnp.where(upper, sz.cx - 1 - plane, plane)


def pack_kernel(
    sz, src_ref, fwd_ref, eps_ref, tiles_ref, freq_ref, mix_ref, pml_ref, *out_refs
):
    inputs = (src_ref, fwd_ref, eps_ref, tiles_ref)
    outs = iter(out_refs)
    for colour in sz.colours:
        top = y_is_high(colour)
        for pairing in (0, 1):
            fill(sz, next(outs), sz.corner, top, from_face(sz, pairing), inputs)
        fill(sz, next(outs), sz.side, top, lambda plane: plane, inputs)
    for pairing in (0, 1):
        fill(sz, next(outs), sz.far, y_is_high(0), from_face(sz, pairing), inputs)
    swap_ref, table_ref = outs

    at_row = lax.broadcasted_iota(jnp.int32, (SUBS, LANES), 0)
    at_lane = lax.broadcasted_iota(jnp.int32, (SUBS, LANES), 1)
    table = jnp.zeros((SUBS, LANES), jnp.float32)
    for row, lane, value in scalars(sz, freq_ref, mix_ref, pml_ref):
        table = jnp.where((at_row == row) & (at_lane == lane), value, table)
    table_ref[...] = table

    _, globally = harmonic_order(sz)
    masks = [kerr_coef * tile_mask(tiles_ref, x, sz.cy) for x in range(sz.cx)]
    for h in range(sz.owned):
        squared = freq_ref[globally(h)] * freq_ref[globally(h)]
        for z in range(sz.halves):
            for x in range(sz.cx):
                inv = 1.0 / (10.0 + squared * eps_ref[x, :, half(z)])
                for r in range(2):
                    for c in range(3):
                        first = src_ref[h, r, c, x, :, half(z)] * inv
                        masked = fwd_ref[h, r, c, x, :, half(z)] * masks[x]
                        swap_ref[0, h, r, c, x, z] = first
                        swap_ref[1, h, r, c, x, z] = masked


def scalars(sz, freq_ref, mix_ref, pml_ref):
    for h in range(sz.harmonics):
        yield 0, h, freq_ref[h] * freq_ref[h]
    for axis in range(3):
        yield 1, axis, pml_ref[axis].astype(jnp.float32)
    for p in range(mix_ref.shape[0]):
        for side in range(2):
            for h in range(sz.harmonics):
                yield 2 + side, p * sz.harmonics + h, mix_ref[p, side, h].astype(jnp.float32)


def relay_kernel(sz, colour, even_ref, odd_ref, anti_ref, main_ref):
    same = x_is_high(0) == y_is_high(colour)

    @pl.when(same)
    def _():
        anti_ref[...] = even_ref[...]
        main_ref[...] = odd_ref[:, : sz.main_rows]

    @pl.when(jnp.logical_not(same))
    def _():
        anti_ref[...] = odd_ref[...]
        main_ref[...] = even_ref[:, : sz.main_rows]


def harmonic_order(sz):
    start = lax.axis_index("ha") * sz.owned
    from_own = lambda index: lax.rem(index - start + sz.harmonics, sz.harmonics)
    globally = lambda position: lax.rem(position + start, sz.harmonics)
    return from_own, globally


def sweep_kernel(sz, mixes, table_ref, eps_ref, *refs):
    cx, cy, cz, halves = sz.cx, sz.cy, sz.cz, sz.halves
    wide, harmonics = sz.wide, sz.harmonics
    blocks, refs = refs[:2], refs[2:]
    per_core = 2 + 5 * len(sz.colours)
    sides = [refs[per_core * s : per_core * (s + 1)] for s in range(sz.ha)]
    out_ref, grad_ref = refs[per_core * sz.ha : per_core * sz.ha + 2]
    base, first, second, fwd, invs, mags, eps_all, table, sem = refs[per_core * sz.ha + 2 :]
    copy = pltpu.make_async_copy(table_ref, table, sem)
    copy.start()

    at_x, at_y = lax.axis_index("gx"), lax.axis_index("gy")
    from_own, globally = harmonic_order(sz)

    nothing = jnp.zeros((DEEP, LANES), jnp.float32)
    low_rows, high_rows = pl.ds(0, DEEP), pl.ds(DEEP + cy, DEEP)
    spots = []
    for x in range(wide):
        for rows in (low_rows, high_rows):
            if len(sz.colours) > 1:
                spots.append((x, rows))
    if len(sz.colours) == 1:
        low = at_y == 0
        there = jnp.where(low, 0, DEEP + cy)
        here = jnp.where(low, DEEP + cy, 0)
        spots += [(x, pl.ds(there, DEEP)) for x in range(wide)]
        corner_at = jnp.where(low, DEEP + cx, 0)
        spots += [(corner_at + d, pl.ds(here, DEEP)) for d in range(DEEP)]
    for x, rows in spots:
        for z in range(halves):
            eps_all[x, z, rows] = nothing
            for g in range(harmonics):
                for r in range(2):
                    for c in range(3):
                        base[g, r, c, x, z, rows] = nothing
                        if isinstance(x, int) and not 1 <= x < wide - 1:
                            continue
                        at = x - 1 if isinstance(x, int) else jnp.clip(x - 1, 0, wide - 3)
                        fwd[g, r, c, at, z, rows] = nothing
    for x in range(wide):
        for z in range(halves):
            eps_all[x, z, sz.rows - 2 :] = jnp.zeros((2, LANES), jnp.float32)
            if DEEP <= x < DEEP + cx:
                eps_all[x, z, DEEP : DEEP + cy] = eps_ref[x - DEEP, :, half(z)]
    copy.wait()

    squared = [table[0, globally(h)] for h in range(harmonics)]
    widths = [table[1, axis].astype(jnp.int32) for axis in range(3)]
    lane = lax.broadcasted_iota(jnp.int32, (SUBS, LANES), 1)
    sub = lax.broadcasted_iota(jnp.int32, (SUBS, LANES), 0)

    def face_spots(pairing, colour):
        high_x, top = x_is_high(pairing), y_is_high(colour)
        plane_of = lambda plane: jnp.where(high_x, DEEP + cx + plane, DEEP - 1 - plane)
        row_of = lambda low, high: jnp.where(top, DEEP + cy - high, DEEP + low)
        return plane_of, row_of

    def side_spots(colour, corner=None):
        high_y = y_is_high(colour)
        if corner is None:
            plane_of = lambda plane: DEEP + plane
        else:
            high_x = jnp.logical_not(high_y) if corner == "anti" else high_y
            plane_of = lambda plane: jnp.where(high_x, DEEP + cx + plane, DEEP - 1 - plane)
        row_of = lambda low, high: jnp.where(high_y, DEEP + cy + low, DEEP - high)
        return plane_of, row_of

    def row_buffers(side):
        buffers = side
        for pairing in (0, 1):
            yield buffers[pairing], sz.far, face_spots(pairing, 0)
        for i, colour in enumerate(sz.colours):
            even, odd, edge, anti, main = buffers[2 + 5 * i : 7 + 5 * i]
            yield even, sz.corner, face_spots(0, colour)
            yield odd, sz.corner, face_spots(1, colour)
            yield edge, sz.side, side_spots(colour)
            yield anti, sz.corner, side_spots(colour, "anti")
            yield main, sz.main, side_spots(colour, "main")

    for buffer, groups, (plane_of, row_of) in row_buffers(sides[0]):
        for field, kind, plane, low, high, at in groups:
            if field == 2:
                for z in range(halves):
                    eps_all[plane_of(plane), z, pl.ds(row_of(low, high), high - low)] = buffer[
                        z, at : at + high - low
                    ]

    def keep_rows(row):
        place = sub + (row - DEEP) + at_y * cy
        return (place >= 0) & (place < cy * sz.gy)

    def keep_plane(x):
        place = x - DEEP + at_x * cx
        return (place >= 0) & (place < cx * sz.gx)

    def scales(x, _):
        inside = jnp.where(keep_plane(x), 1.0, 0.0)
        for row in (0, SUBS):
            keep = jnp.where(keep_rows(row), inside, 0.0)
            for z in range(halves):
                eps = eps_all[x, z, row : row + SUBS]
                for h in range(harmonics):
                    invs[h, x, z, row : row + SUBS] = keep / (10.0 + squared[h] * eps)
        return 0

    lax.fori_loop(0, wide, scales, 0)

    for s, block in enumerate(blocks):
        for h, r, c in sz.kinds:
            g = s * sz.owned + h
            for x in range(cx):
                for z in range(halves):
                    rows = slice(DEEP, DEEP + cy)
                    base[g, r, c, DEEP + x, z, rows] = block[0, h, r, c, x, z]
                    fwd[g, r, c, NEAR + x, z, rows] = block[1, h, r, c, x, z]
    for s, side in enumerate(sides):
        for buffer, groups, (plane_of, row_of) in row_buffers(side):
            for field, kind, plane, low, high, at in groups:
                if field == 2:
                    continue
                h, r, c = kind
                g = s * sz.owned + h
                x, rows = plane_of(plane), pl.ds(row_of(low, high), high - low)
                for z in range(halves):
                    got = buffer[z, at : at + high - low]
                    if field == 0:
                        base[g, r, c, x, z, rows] = got * invs[g, x, z, rows]
                    else:
                        fwd[g, r, c, x - 1, z, rows] = got

    def profile(width, place, cells):
        reach = jnp.maximum(jnp.maximum(width - place, place - (cells - 1 - width)), 0)
        return (reach.astype(jnp.float32) / jnp.full(reach.shape, width).astype(jnp.float32)) ** 2

    sigma_z = [profile(widths[2], lane + z * LANES, cz) for z in range(halves)]

    def z_ahead(parts):
        turned = [pltpu.roll(v, LANES - 1, 1) for v in parts]
        following = turned[1:] + [0.0]
        return [jnp.where(lane == LANES - 1, f, t) for t, f in zip(turned, following)]

    def z_behind(parts):
        turned = [pltpu.roll(v, 1, 1) for v in parts]
        previous = [0.0] + turned[:-1]
        return [jnp.where(lane == 0, p, t) for t, p in zip(turned, previous)]

    def mixed(side, h, p):
        return from_own(table[2 + side, p * harmonics + globally(h)].astype(jnp.int32))

    pairs = [(mixed(0, h, p), mixed(1, h, p)) for h in range(harmonics) for p in range(mixes)]
    zs = range(halves)

    def sweep(k, v_ref, store):
        lo, hi = k + 1, wide - 1 - k
        top = DEEP + cy + NEAR - k
        out_rows = sorted({k + 1, top - SUBS})
        mag_rows = sorted({k, top - SUBS})
        sigma_y = {
            row: profile(widths[1], sub + (row - DEEP) + at_y * cy, cy * sz.gy) for row in out_rows
        }

        def write_mags(x, g, comps):
            slot = lax.rem(x, 2)
            inside = x - DEEP + at_x * cx >= 0
            for r in range(2):
                for row in mag_rows:
                    mask = (sub + (row - DEEP) + at_y * cy >= 0) & inside
                    fx, fy, fz = [
                        [v_ref[g, r, c, x, z, row : row + SUBS] for z in zs] for c in range(3)
                    ]
                    next_y, next_z = [
                        [v_ref[g, r, c, x + 1, z, row : row + SUBS] for z in zs] for c in (1, 2)
                    ]
                    above_x, above_z = [
                        [v_ref[g, r, c, x, z, row + 1 : row + 1 + SUBS] for z in zs] for c in (0, 2)
                    ]
                    after_x = z_ahead(fx)
                    found = {}
                    if 0 in comps:
                        after_y = z_ahead(fy)
                        found[0] = [(above_z[z] - fz[z]) - (after_y[z] - fy[z]) for z in zs]
                    found[1] = [(after_x[z] - fx[z]) - (next_z[z] - fz[z]) for z in zs]
                    found[2] = [(next_y[z] - fy[z]) - (above_x[z] - fx[z]) for z in zs]
                    for c, parts in found.items():
                        for z in zs:
                            pltpu.store(
                                mags.at[slot, g, r, c, z, row : row + SUBS], parts[z], mask=mask
                            )

        for slot in range(2):
            for g in range(harmonics):
                for r in range(2):
                    for c in range(3):
                        for z in zs:
                            mags[slot, g, r, c, z] = jnp.zeros((sz.rows, LANES), jnp.float32)
        for g in range(harmonics):
            write_mags(k, g, (1, 2))

        def body(x, _):
            slot, past = lax.rem(x, 2), lax.rem(x + 1, 2)
            twice = jnp.where(keep_plane(x), 2.0, 0.0)
            place = jnp.full((SUBS, LANES), x - DEEP + at_x * cx)
            sigma_x = profile(widths[0], place, cx * sz.gx)
            spots = [(row, z) for row in out_rows for z in zs]
            sigma = {
                (row, z): sigma_peak * (sigma_x + sigma_y[row] + sigma_z[z]) for row, z in spots
            }
            double = {row: jnp.where(keep_rows(row), twice, 0.0) for row in out_rows}
            for h in range(harmonics):
                write_mags(x, h, (0, 1, 2))
                curls = {}
                for row in out_rows:
                    span, below = slice(row, row + SUBS), slice(row - 1, row - 1 + SUBS)
                    for r in range(2):
                        mag = [[mags[slot, h, r, c, z, span] for z in zs] for c in range(3)]
                        low_x, low_z = [
                            [mags[slot, h, r, c, z, below] for z in zs] for c in (0, 2)
                        ]
                        past_y, past_z = [
                            [mags[past, h, r, c, z, span] for z in zs] for c in (1, 2)
                        ]
                        before_x, before_y = z_behind(mag[0]), z_behind(mag[1])
                        for z in zs:
                            curls[row, z, r] = [
                                (mag[2][z] - low_z[z]) - (mag[1][z] - before_y[z]),
                                (mag[0][z] - before_x[z]) - (mag[2][z] - past_z[z]),
                                (mag[1][z] - past_y[z]) - (mag[0][z] - low_x[z]),
                            ]
                inv = {(row, z): invs[h, x, z, row : row + SUBS] for row, z in spots}
                slope = {(row, z): double[row] - 10.0 * inv[row, z] for row, z in spots}
                absorb = {spot: squared[h] * sigma[spot] for spot in spots}
                for c in range(3):
                    real, imag = {}, {}
                    for p in range(mixes):
                        a, b = pairs[h * mixes + p]
                        for row, z in spots:
                            span = slice(row, row + SUBS)
                            fr, fi = [fwd[a, r, c, x - 1, z, span] for r in range(2)]
                            vr, vi = [v_ref[b, r, c, x, z, span] for r in range(2)]
                            one, two = fr * vr - fi * vi, fr * vi + fi * vr
                            real[row, z] = real[row, z] + one if p else one
                            imag[row, z] = imag[row, z] + two if p else two
                    for row, z in spots:
                        span = slice(row, row + SUBS)
                        vr, vi = [v_ref[h, r, c, x, z, span] for r in range(2)]
                        new_r = (
                            base[h, 0, c, x, z, span]
                            + vr * slope[row, z]
                            + inv[row, z]
                            * (squared[h] * real[row, z] - absorb[row, z] * vi - curls[row, z, 0][c])
                        )
                        new_i = (
                            base[h, 1, c, x, z, span]
                            + vi * slope[row, z]
                            + inv[row, z]
                            * (squared[h] * imag[row, z] + absorb[row, z] * vr - curls[row, z, 1][c])
                        )
                        store(h, c, x, z, span, new_r, new_i)
            return 0

        lax.fori_loop(lo, hi, body, 0)

    def store_in(ref):
        def store(h, c, x, z, span, new_r, new_i):
            ref[h, 0, c, x, z, span] = new_r
            ref[h, 1, c, x, z, span] = new_i

        return store

    sums = {}

    def store_out(h, c, x, z, span, new_r, new_i):
        if h < sz.owned:
            out_ref[h, 0, c, x - DEEP, :, half(z)] = new_r
            out_ref[h, 1, c, x - DEEP, :, half(z)] = new_i
        term = (squared[h] / kerr_coef) * (
            new_r * fwd[h, 0, c, x - 1, z, span] - new_i * fwd[h, 1, c, x - 1, z, span]
        )
        if h == 0 and c == 0:
            sums[z] = term
        else:
            sums[z] = sums[z] + term
        if h == harmonics - 1 and c == 2:
            grad_ref[x - DEEP, :, half(z)] = sums[z]

    sweep(0, base, store_in(first))
    sweep(1, first, store_in(second))
    sweep(2, second, store_out)


def swaps(count_x, count_y, partner):
    sends = []
    for x in range(count_x):
        for y in range(count_y):
            to_x, to_y = partner(x, y)
            if 0 <= to_x < count_x and 0 <= to_y < count_y:
                sends.append((x * count_y + y, to_x * count_y + to_y))
    return sends


def shards(
    forward_field, adjoint_source, permittivity, frequency, design_tiles, mix_pairs, pml_width
):
    counts = tuple(lax.axis_size(name) for name in ("gx", "gy", "ha"))
    sz = Sizes(forward_field.shape[0], permittivity.shape, counts)
    f32 = jnp.float32

    def rows_buffer(rows):
        return jax.ShapeDtypeStruct((sz.halves, round_up(rows), LANES), f32)

    def field(planes):
        return pltpu.VMEM((sz.harmonics, 2, 3, planes, sz.halves, sz.rows, LANES), f32)

    swapped = jax.ShapeDtypeStruct((2, sz.owned, 2, 3, sz.cx, sz.halves, sz.cy, LANES), f32)

    def send(buffer, partner):
        return lax.ppermute(buffer, ("gx", "gy"), swaps(sz.gx, sz.gy, partner))

    def step(place, colour):
        return 1 if (place + colour) % 2 == 0 else -1

    def along_x(buffer, pairing):
        return send(buffer, lambda x, y: (x + step(x, pairing), y))

    def along_y(buffer, colour):
        return send(buffer, lambda x, y: (x, y + step(y, colour)))

    corner, edge = rows_buffer(sz.corner_rows), rows_buffer(sz.side_rows)
    mix_by_pair = jnp.transpose(mix_pairs, (1, 2, 0))
    far_buf, table = rows_buffer(sz.far_rows), jax.ShapeDtypeStruct((SUBS, LANES), f32)
    shapes = [corner, corner, edge] * len(sz.colours)
    shapes += [far_buf, far_buf, swapped, table]
    packed = pl.pallas_call(
        functools.partial(pack_kernel, sz),
        out_shape=shapes,
        in_specs=[VMEM] * 3 + [SMEM] * 4,
        out_specs=[VMEM] * len(shapes),
        name="pack",
    )(adjoint_source, forward_field, permittivity, design_tiles, frequency, mix_by_pair, pml_width)
    near = packed[: 3 * len(sz.colours)]
    *far, mine, table = packed[3 * len(sz.colours) :]
    got = []
    for i, colour in enumerate(sz.colours):
        even = along_x(near[3 * i], 0)
        odd = along_x(near[3 * i + 1], 1)
        side = along_y(near[3 * i + 2], colour)
        anti, main = pl.pallas_call(
            functools.partial(relay_kernel, sz, colour),
            out_shape=[corner, rows_buffer(sz.main_rows)],
            in_specs=[VMEM, VMEM],
            out_specs=[VMEM, VMEM],
            compiler_params=pltpu.CompilerParams(vmem_limit_bytes=4 * 1024 * 1024),
            name="relay",
        )(even, odd)
        anti = along_y(anti, colour)
        main = along_y(main, colour)
        got += [even, odd, side, anti, main]
    far_even = along_x(far[0], 0)
    far_odd = along_x(far[1], 1)
    own = [mine, far_even, far_odd] + got
    flip = [(i, sz.ha - 1 - i) for i in range(sz.ha)]
    other = []
    for buffer in own:
        other.append(lax.ppermute(buffer, "ha", flip))

    buffers = own[:1] + other[:1] + own[1:] + other[1:]
    adjoint, gradient = pl.pallas_call(
        functools.partial(sweep_kernel, sz, mix_pairs.shape[1]),
        out_shape=[
            jax.ShapeDtypeStruct(adjoint_source.shape, f32),
            jax.ShapeDtypeStruct(permittivity.shape, f32),
        ],
        in_specs=[VMEM] * (2 + len(buffers)),
        out_specs=[VMEM] * 2,
        scratch_shapes=[
            field(sz.wide),
            field(sz.wide),
            field(sz.wide),
            field(sz.wide - 2),
            pltpu.VMEM((sz.harmonics, sz.wide, sz.halves, sz.rows, LANES), f32),
            pltpu.VMEM((2, sz.harmonics, 2, 3, sz.halves, sz.rows, LANES), f32),
            pltpu.VMEM((sz.wide, sz.halves, sz.rows, LANES), f32),
            pltpu.SMEM((SUBS, LANES), f32),
            pltpu.SemaphoreType.DMA,
        ],
        compiler_params=pltpu.CompilerParams(vmem_limit_bytes=32 * 1024 * 1024),
        name="sweeps",
    )(table, permittivity, *buffers)
    return (adjoint, gradient)


def solution(mesh):
    return jax.shard_map(
        shards,
        mesh=mesh,
        in_specs=(
            P("ha", None, None, ("cand", "gx"), "gy", None),
            P("ha", None, None, ("cand", "gx"), "gy", None),
            P(("cand", "gx"), "gy", None),
            P(),
            P(("cand", "gx"), "gy"),
            P(),
            P(),
        ),
        out_specs=(P("ha", None, None, ("cand", "gx"), "gy", None), P(("cand", "gx"), "gy", None)),
        check_vma=False,
    )
```

```python
import functools

import jax
import jax.numpy as jnp
from jax import lax
from jax.experimental import pallas as pl
from jax.experimental.pallas import tpu as pltpu
from jax.sharding import PartitionSpec as P


ITERS = 3
TILE = 4
DEEP = ITERS
NEAR = ITERS - 1
LANES = 128
SUBS = 8

kerr_coef = 4.0
sigma_peak = 8.0

VMEM = pl.BlockSpec(memory_space=pltpu.VMEM)
SMEM = pl.BlockSpec(memory_space=pltpu.SMEM)


class Sizes:
    def __init__(self, owned, cells, counts):
        self.owned = owned
        self.cx, self.cy, self.cz = cells
        self.gx, self.gy, self.ha = counts
        self.harmonics = owned * self.ha
        self.halves = self.cz // LANES
        self.wide = self.cx + 2 * DEEP
        self.rows = self.cy + 2 * DEEP + 2
        self.kinds = [(h, r, c) for h in range(owned) for r in range(2) for c in range(3)]
        self.colours = (0,) if self.gy == 2 else (0, 1)
        assert self.cy == SUBS and self.cx >= DEEP
        planes = range(self.cx)
        self.side, self.side_rows = self.groups(
            [(x, 0, DEEP) for x in planes], [(x, 0, NEAR) for x in planes]
        )
        self.main, at = self.groups(
            [(p, 0, DEEP - 1 - p) for p in range(DEEP - 1)],
            [(p, 0, NEAR - 1 - p) for p in range(NEAR - 1)],
        )
        rest, self.corner_rows = self.groups(
            [(p, DEEP - 1 - p, DEEP) for p in range(DEEP)],
            [(p, NEAR - 1 - p, NEAR) for p in range(NEAR)],
            at,
        )
        self.corner = self.main + rest
        self.main_rows = round_up(at)
        edges = len(self.colours) - 1
        self.far, self.far_rows = self.groups(
            [(p, DEEP, self.cy - edges * DEEP) for p in range(DEEP)],
            [(p, NEAR, self.cy - edges * NEAR) for p in range(NEAR)],
        )

    def groups(self, deep, near, at=SUBS):
        listed = []
        for field, kinds, planes in ((0, self.kinds, deep), (1, self.kinds, near), (2, [()], deep)):
            for kind in kinds:
                for plane, low, high in planes:
                    listed.append((field, kind, plane, low, high, at))
                    at += high - low
        return listed, at


def round_up(rows):
    return (rows + SUBS - 1) // SUBS * SUBS


def half(z):
    return slice(z * LANES, (z + 1) * LANES)


def tile_mask(tiles_ref, plane, rows):
    place = lax.broadcasted_iota(jnp.int32, (rows, LANES), 0) // TILE
    mask = jnp.zeros((rows, LANES), jnp.float32)
    for col in range(rows // TILE):
        cell = tiles_ref[plane // TILE, col].astype(jnp.float32)
        mask = jnp.where(place == col, cell, mask)
    return mask


def plane_mask(tiles_ref, plane, sz):
    mask = tile_mask(tiles_ref, 0, sz.cy)
    for x in range(TILE, sz.cx, TILE):
        mask = jnp.where(plane >= x, tile_mask(tiles_ref, x, sz.cy), mask)
    return kerr_coef * mask


def x_is_high(colour):
    return lax.rem(lax.axis_index("gx") + colour, 2) == 0


def y_is_high(colour):
    return lax.rem(lax.axis_index("gy") + colour, 2) == 0


def fill(sz, ref, groups, top, plane_of, inputs):
    src_ref, fwd_ref, eps_ref, tiles_ref = inputs
    mask = plane_mask(tiles_ref, 0, sz) if sz.cx <= TILE else None
    for field, kind, plane, low, high, at in reversed(groups):
        x = plane_of(plane)
        room = sz.cy - (high - low)
        for z in range(sz.halves):
            if field == 2:
                tile = eps_ref[x, :, half(z)]
            elif field == 0:
                tile = src_ref[(*kind, x, slice(None), half(z))]
            else:
                scale = plane_mask(tiles_ref, x, sz) if mask is None else mask
                tile = fwd_ref[(*kind, x, slice(None), half(z))] * scale
            if_top = pltpu.roll(tile, low, 0) if low else tile
            if_not = pltpu.roll(tile, sz.cy - high, 0) if high < sz.cy else tile
            ref[z, at - room : at + high - low] = jnp.where(top, if_top, if_not)


def from_face(sz, colour):
    upper = x_is_high(colour)
    return lambda plane: jnp.where(upper, sz.cx - 1 - plane, plane)


def pack_kernel(
    sz, src_ref, fwd_ref, eps_ref, tiles_ref, freq_ref, mix_ref, pml_ref, *out_refs
):
    inputs = (src_ref, fwd_ref, eps_ref, tiles_ref)
    outs = iter(out_refs)
    for colour in sz.colours:
        top = y_is_high(colour)
        for pairing in (0, 1):
            fill(sz, next(outs), sz.corner, top, from_face(sz, pairing), inputs)
        fill(sz, next(outs), sz.side, top, lambda plane: plane, inputs)
    for pairing in (0, 1):
        fill(sz, next(outs), sz.far, y_is_high(0), from_face(sz, pairing), inputs)
    swap_ref, table_ref = outs

    at_row = lax.broadcasted_iota(jnp.int32, (SUBS, LANES), 0)
    at_lane = lax.broadcasted_iota(jnp.int32, (SUBS, LANES), 1)
    table = jnp.zeros((SUBS, LANES), jnp.float32)
    for row, lane, value in scalars(sz, freq_ref, mix_ref, pml_ref, tiles_ref):
        table = jnp.where((at_row == row) & (at_lane == lane), value, table)
    table_ref[...] = table

    _, globally = harmonic_order(sz)
    masks = [kerr_coef * tile_mask(tiles_ref, x, sz.cy) for x in range(sz.cx)]
    for h in range(sz.owned):
        squared = freq_ref[globally(h)] * freq_ref[globally(h)]
        for z in range(sz.halves):
            for x in range(sz.cx):
                inv = 1.0 / (10.0 + squared * eps_ref[x, :, half(z)])
                for r in range(2):
                    for c in range(3):
                        first = src_ref[h, r, c, x, :, half(z)] * inv
                        masked = fwd_ref[h, r, c, x, :, half(z)] * masks[x]
                        swap_ref[0, h, r, c, x, z] = first
                        swap_ref[1, h, r, c, x, z] = masked


def scalars(sz, freq_ref, mix_ref, pml_ref, tiles_ref):
    for h in range(sz.harmonics):
        yield 0, h, freq_ref[h] * freq_ref[h]
    for axis in range(3):
        yield 1, axis, pml_ref[axis].astype(jnp.float32)
    for p in range(mix_ref.shape[0]):
        for side in range(2):
            for h in range(sz.harmonics):
                yield 2 + side, p * sz.harmonics + h, mix_ref[p, side, h].astype(jnp.float32)
    cols = sz.cy // TILE
    for row in range(sz.cx // TILE):
        for col in range(cols):
            yield 4, row * cols + col, tiles_ref[row, col].astype(jnp.float32)


def relay_kernel(sz, colour, even_ref, odd_ref, anti_ref, main_ref):
    same = x_is_high(0) == y_is_high(colour)

    @pl.when(same)
    def _():
        anti_ref[...] = even_ref[...]
        main_ref[...] = odd_ref[:, : sz.main_rows]

    @pl.when(jnp.logical_not(same))
    def _():
        anti_ref[...] = odd_ref[...]
        main_ref[...] = even_ref[:, : sz.main_rows]


def harmonic_order(sz):
    start = lax.axis_index("ha") * sz.owned
    from_own = lambda index: lax.rem(index - start + sz.harmonics, sz.harmonics)
    globally = lambda position: lax.rem(position + start, sz.harmonics)
    return from_own, globally


def sweep_kernel(sz, mixes, table_ref, eps_ref, *refs):
    cx, cy, cz, halves = sz.cx, sz.cy, sz.cz, sz.halves
    wide, harmonics = sz.wide, sz.harmonics
    src_ref, fwd_ref, theirs = refs[:3]
    refs = refs[3:]
    per_core = 2 + 5 * len(sz.colours)
    sides = [refs[per_core * s : per_core * (s + 1)] for s in range(sz.ha)]
    out_ref, grad_ref = refs[per_core * sz.ha : per_core * sz.ha + 2]
    base, first, second, fwd, invs, mags, eps_all, table, sem = refs[per_core * sz.ha + 2 :]
    copy = pltpu.make_async_copy(table_ref, table, sem)
    copy.start()

    at_x, at_y = lax.axis_index("gx"), lax.axis_index("gy")
    from_own, globally = harmonic_order(sz)

    nothing = jnp.zeros((DEEP, LANES), jnp.float32)
    low_rows, high_rows = pl.ds(0, DEEP), pl.ds(DEEP + cy, DEEP)
    spots = []
    for x in range(wide):
        for rows in (low_rows, high_rows):
            if len(sz.colours) > 1:
                spots.append((x, rows))
    if len(sz.colours) == 1:
        low = at_y == 0
        there = jnp.where(low, 0, DEEP + cy)
        here = jnp.where(low, DEEP + cy, 0)
        spots += [(x, pl.ds(there, DEEP)) for x in range(wide)]
        corner_at = jnp.where(low, DEEP + cx, 0)
        spots += [(corner_at + d, pl.ds(here, DEEP)) for d in range(DEEP)]
    for x, rows in spots:
        for z in range(halves):
            eps_all[x, z, rows] = nothing
            for g in range(harmonics):
                for r in range(2):
                    for c in range(3):
                        base[g, r, c, x, z, rows] = nothing
                        if isinstance(x, int) and not 1 <= x < wide - 1:
                            continue
                        at = x - 1 if isinstance(x, int) else jnp.clip(x - 1, 0, wide - 3)
                        fwd[g, r, c, at, z, rows] = nothing
    for x in range(wide):
        for z in range(halves):
            eps_all[x, z, sz.rows - 2 :] = jnp.zeros((2, LANES), jnp.float32)
            if DEEP <= x < DEEP + cx:
                eps_all[x, z, DEEP : DEEP + cy] = eps_ref[x - DEEP, :, half(z)]
    copy.wait()

    squared = [table[0, globally(h)] for h in range(harmonics)]
    widths = [table[1, axis].astype(jnp.int32) for axis in range(3)]
    lane = lax.broadcasted_iota(jnp.int32, (SUBS, LANES), 1)
    sub = lax.broadcasted_iota(jnp.int32, (SUBS, LANES), 0)

    def face_spots(pairing, colour):
        high_x, top = x_is_high(pairing), y_is_high(colour)
        plane_of = lambda plane: jnp.where(high_x, DEEP + cx + plane, DEEP - 1 - plane)
        row_of = lambda low, high: jnp.where(top, DEEP + cy - high, DEEP + low)
        return plane_of, row_of

    def side_spots(colour, corner=None):
        high_y = y_is_high(colour)
        if corner is None:
            plane_of = lambda plane: DEEP + plane
        else:
            high_x = jnp.logical_not(high_y) if corner == "anti" else high_y
            plane_of = lambda plane: jnp.where(high_x, DEEP + cx + plane, DEEP - 1 - plane)
        row_of = lambda low, high: jnp.where(high_y, DEEP + cy + low, DEEP - high)
        return plane_of, row_of

    def row_buffers(side):
        buffers = side
        for pairing in (0, 1):
            yield buffers[pairing], sz.far, face_spots(pairing, 0)
        for i, colour in enumerate(sz.colours):
            even, odd, edge, anti, main = buffers[2 + 5 * i : 7 + 5 * i]
            yield even, sz.corner, face_spots(0, colour)
            yield odd, sz.corner, face_spots(1, colour)
            yield edge, sz.side, side_spots(colour)
            yield anti, sz.corner, side_spots(colour, "anti")
            yield main, sz.main, side_spots(colour, "main")

    for buffer, groups, (plane_of, row_of) in row_buffers(sides[0]):
        for field, kind, plane, low, high, at in groups:
            if field == 2:
                for z in range(halves):
                    eps_all[plane_of(plane), z, pl.ds(row_of(low, high), high - low)] = buffer[
                        z, at : at + high - low
                    ]

    def keep_rows(row):
        place = sub + (row - DEEP) + at_y * cy
        return (place >= 0) & (place < cy * sz.gy)

    def keep_plane(x):
        place = x - DEEP + at_x * cx
        return (place >= 0) & (place < cx * sz.gx)

    def scales(x, _):
        inside = jnp.where(keep_plane(x), 1.0, 0.0)
        for row in (0, SUBS):
            keep = jnp.where(keep_rows(row), inside, 0.0)
            for z in range(halves):
                eps = eps_all[x, z, row : row + SUBS]
                for h in range(harmonics):
                    invs[h, x, z, row : row + SUBS] = keep / (10.0 + squared[h] * eps)
        return 0

    lax.fori_loop(0, wide, scales, 0)

    rows = slice(DEEP, DEEP + cy)
    place = lax.broadcasted_iota(jnp.int32, (cy, LANES), 0) // TILE
    cols = cy // TILE
    for x in range(cx):
        mask = jnp.zeros((cy, LANES), jnp.float32)
        for col in range(cols):
            mask = jnp.where(place == col, kerr_coef * table[4, x // TILE * cols + col], mask)
        for h, r, c in sz.kinds:
            g = sz.owned + h
            for z in range(halves):
                base[h, r, c, DEEP + x, z, rows] = (
                    src_ref[h, r, c, x, :, half(z)] * invs[h, DEEP + x, z, rows]
                )
                fwd[h, r, c, NEAR + x, z, rows] = fwd_ref[h, r, c, x, :, half(z)] * mask
                base[g, r, c, DEEP + x, z, rows] = theirs[0, h, r, c, x, z]
                fwd[g, r, c, NEAR + x, z, rows] = theirs[1, h, r, c, x, z]
    for s, side in enumerate(sides):
        for buffer, groups, (plane_of, row_of) in row_buffers(side):
            for field, kind, plane, low, high, at in groups:
                if field == 2:
                    continue
                h, r, c = kind
                g = s * sz.owned + h
                x, rows = plane_of(plane), pl.ds(row_of(low, high), high - low)
                for z in range(halves):
                    got = buffer[z, at : at + high - low]
                    if field == 0:
                        base[g, r, c, x, z, rows] = got * invs[g, x, z, rows]
                    else:
                        fwd[g, r, c, x - 1, z, rows] = got

    def profile(width, place, cells):
        reach = jnp.maximum(jnp.maximum(width - place, place - (cells - 1 - width)), 0)
        return (reach.astype(jnp.float32) / jnp.full(reach.shape, width).astype(jnp.float32)) ** 2

    sigma_z = [profile(widths[2], lane + z * LANES, cz) for z in range(halves)]

    def z_ahead(parts):
        turned = [pltpu.roll(v, LANES - 1, 1) for v in parts]
        following = turned[1:] + [0.0]
        return [jnp.where(lane == LANES - 1, f, t) for t, f in zip(turned, following)]

    def z_behind(parts):
        turned = [pltpu.roll(v, 1, 1) for v in parts]
        previous = [0.0] + turned[:-1]
        return [jnp.where(lane == 0, p, t) for t, p in zip(turned, previous)]

    def mixed(side, h, p):
        return from_own(table[2 + side, p * harmonics + globally(h)].astype(jnp.int32))

    pairs = [(mixed(0, h, p), mixed(1, h, p)) for h in range(harmonics) for p in range(mixes)]
    zs = range(halves)

    def sweep(k, v_ref, store):
        lo, hi = k + 1, wide - 1 - k
        top = DEEP + cy + NEAR - k
        out_rows = sorted({k + 1, top - SUBS})
        mag_rows = sorted({k, top - SUBS})
        sigma_y = {
            row: profile(widths[1], sub + (row - DEEP) + at_y * cy, cy * sz.gy) for row in out_rows
        }

        def write_mags(x, g, comps):
            slot = lax.rem(x, 2)
            inside = x - DEEP + at_x * cx >= 0
            for r in range(2):
                for row in mag_rows:
                    mask = (sub + (row - DEEP) + at_y * cy >= 0) & inside
                    fx, fy, fz = [
                        [v_ref[g, r, c, x, z, row : row + SUBS] for z in zs] for c in range(3)
                    ]
                    next_y, next_z = [
                        [v_ref[g, r, c, x + 1, z, row : row + SUBS] for z in zs] for c in (1, 2)
                    ]
                    above_x, above_z = [
                        [v_ref[g, r, c, x, z, row + 1 : row + 1 + SUBS] for z in zs] for c in (0, 2)
                    ]
                    after_x = z_ahead(fx)
                    found = {}
                    if 0 in comps:
                        after_y = z_ahead(fy)
                        found[0] = [(above_z[z] - fz[z]) - (after_y[z] - fy[z]) for z in zs]
                    found[1] = [(after_x[z] - fx[z]) - (next_z[z] - fz[z]) for z in zs]
                    found[2] = [(next_y[z] - fy[z]) - (above_x[z] - fx[z]) for z in zs]
                    for c, parts in found.items():
                        for z in zs:
                            pltpu.store(
                                mags.at[slot, g, r, c, z, row : row + SUBS], parts[z], mask=mask
                            )

        for slot in range(2):
            for g in range(harmonics):
                for r in range(2):
                    for c in range(3):
                        for z in zs:
                            mags[slot, g, r, c, z] = jnp.zeros((sz.rows, LANES), jnp.float32)
        for g in range(harmonics):
            write_mags(k, g, (1, 2))

        def body(x, _):
            slot, past = lax.rem(x, 2), lax.rem(x + 1, 2)
            twice = jnp.where(keep_plane(x), 2.0, 0.0)
            place = jnp.full((SUBS, LANES), x - DEEP + at_x * cx)
            sigma_x = profile(widths[0], place, cx * sz.gx)
            spots = [(row, z) for row in out_rows for z in zs]
            sigma = {
                (row, z): sigma_peak * (sigma_x + sigma_y[row] + sigma_z[z]) for row, z in spots
            }
            double = {row: jnp.where(keep_rows(row), twice, 0.0) for row in out_rows}
            for h in range(harmonics):
                write_mags(x, h, (0, 1, 2))
                curls = {}
                for row in out_rows:
                    span, below = slice(row, row + SUBS), slice(row - 1, row - 1 + SUBS)
                    for r in range(2):
                        mag = [[mags[slot, h, r, c, z, span] for z in zs] for c in range(3)]
                        low_x, low_z = [
                            [mags[slot, h, r, c, z, below] for z in zs] for c in (0, 2)
                        ]
                        past_y, past_z = [
                            [mags[past, h, r, c, z, span] for z in zs] for c in (1, 2)
                        ]
                        before_x, before_y = z_behind(mag[0]), z_behind(mag[1])
                        for z in zs:
                            curls[row, z, r] = [
                                (mag[2][z] - low_z[z]) - (mag[1][z] - before_y[z]),
                                (mag[0][z] - before_x[z]) - (mag[2][z] - past_z[z]),
                                (mag[1][z] - past_y[z]) - (mag[0][z] - low_x[z]),
                            ]
                inv = {(row, z): invs[h, x, z, row : row + SUBS] for row, z in spots}
                slope = {(row, z): double[row] - 10.0 * inv[row, z] for row, z in spots}
                absorb = {spot: squared[h] * sigma[spot] for spot in spots}
                for c in range(3):
                    real, imag = {}, {}
                    for p in range(mixes):
                        a, b = pairs[h * mixes + p]
                        for row, z in spots:
                            span = slice(row, row + SUBS)
                            fr, fi = [fwd[a, r, c, x - 1, z, span] for r in range(2)]
                            vr, vi = [v_ref[b, r, c, x, z, span] for r in range(2)]
                            one, two = fr * vr - fi * vi, fr * vi + fi * vr
                            real[row, z] = real[row, z] + one if p else one
                            imag[row, z] = imag[row, z] + two if p else two
                    for row, z in spots:
                        span = slice(row, row + SUBS)
                        vr, vi = [v_ref[h, r, c, x, z, span] for r in range(2)]
                        new_r = (
                            base[h, 0, c, x, z, span]
                            + vr * slope[row, z]
                            + inv[row, z]
                            * (squared[h] * real[row, z] - absorb[row, z] * vi - curls[row, z, 0][c])
                        )
                        new_i = (
                            base[h, 1, c, x, z, span]
                            + vi * slope[row, z]
                            + inv[row, z]
                            * (squared[h] * imag[row, z] + absorb[row, z] * vr - curls[row, z, 1][c])
                        )
                        store(h, c, x, z, span, new_r, new_i)
            return 0

        lax.fori_loop(lo, hi, body, 0)

    def store_in(ref):
        def store(h, c, x, z, span, new_r, new_i):
            ref[h, 0, c, x, z, span] = new_r
            ref[h, 1, c, x, z, span] = new_i

        return store

    sums = {}

    def store_out(h, c, x, z, span, new_r, new_i):
        if h < sz.owned:
            out_ref[h, 0, c, x - DEEP, :, half(z)] = new_r
            out_ref[h, 1, c, x - DEEP, :, half(z)] = new_i
        term = (squared[h] / kerr_coef) * (
            new_r * fwd[h, 0, c, x - 1, z, span] - new_i * fwd[h, 1, c, x - 1, z, span]
        )
        if h == 0 and c == 0:
            sums[z] = term
        else:
            sums[z] = sums[z] + term
        if h == harmonics - 1 and c == 2:
            grad_ref[x - DEEP, :, half(z)] = sums[z]

    sweep(0, base, store_in(first))
    sweep(1, first, store_in(second))
    sweep(2, second, store_out)


def swaps(count_x, count_y, partner):
    sends = []
    for x in range(count_x):
        for y in range(count_y):
            to_x, to_y = partner(x, y)
            if 0 <= to_x < count_x and 0 <= to_y < count_y:
                sends.append((x * count_y + y, to_x * count_y + to_y))
    return sends


def shards(
    forward_field, adjoint_source, permittivity, frequency, design_tiles, mix_pairs, pml_width
):
    counts = tuple(lax.axis_size(name) for name in ("gx", "gy", "ha"))
    sz = Sizes(forward_field.shape[0], permittivity.shape, counts)
    f32 = jnp.float32

    def rows_buffer(rows):
        return jax.ShapeDtypeStruct((sz.halves, round_up(rows), LANES), f32)

    def field(planes):
        return pltpu.VMEM((sz.harmonics, 2, 3, planes, sz.halves, sz.rows, LANES), f32)

    swapped = jax.ShapeDtypeStruct((2, sz.owned, 2, 3, sz.cx, sz.halves, sz.cy, LANES), f32)

    def send(buffer, partner):
        return lax.ppermute(buffer, ("gx", "gy"), swaps(sz.gx, sz.gy, partner))

    def step(place, colour):
        return 1 if (place + colour) % 2 == 0 else -1

    def along_x(buffer, pairing):
        return send(buffer, lambda x, y: (x + step(x, pairing), y))

    def along_y(buffer, colour):
        return send(buffer, lambda x, y: (x, y + step(y, colour)))

    corner, edge = rows_buffer(sz.corner_rows), rows_buffer(sz.side_rows)
    mix_by_pair = jnp.transpose(mix_pairs, (1, 2, 0))
    far_buf, table = rows_buffer(sz.far_rows), jax.ShapeDtypeStruct((SUBS, LANES), f32)
    shapes = [corner, corner, edge] * len(sz.colours)
    shapes += [far_buf, far_buf, swapped, table]
    packed = pl.pallas_call(
        functools.partial(pack_kernel, sz),
        out_shape=shapes,
        in_specs=[VMEM] * 3 + [SMEM] * 4,
        out_specs=[VMEM] * len(shapes),
        name="pack",
    )(adjoint_source, forward_field, permittivity, design_tiles, frequency, mix_by_pair, pml_width)
    near = packed[: 3 * len(sz.colours)]
    *far, mine, table = packed[3 * len(sz.colours) :]
    got = []
    for i, colour in enumerate(sz.colours):
        even = along_x(near[3 * i], 0)
        odd = along_x(near[3 * i + 1], 1)
        side = along_y(near[3 * i + 2], colour)
        anti, main = pl.pallas_call(
            functools.partial(relay_kernel, sz, colour),
            out_shape=[corner, rows_buffer(sz.main_rows)],
            in_specs=[VMEM, VMEM],
            out_specs=[VMEM, VMEM],
            compiler_params=pltpu.CompilerParams(vmem_limit_bytes=4 * 1024 * 1024),
            name="relay",
        )(even, odd)
        anti = along_y(anti, colour)
        main = along_y(main, colour)
        got += [even, odd, side, anti, main]
    far_even = along_x(far[0], 0)
    far_odd = along_x(far[1], 1)
    own = [mine, far_even, far_odd] + got
    flip = [(i, sz.ha - 1 - i) for i in range(sz.ha)]
    other = []
    for buffer in own:
        other.append(lax.ppermute(buffer, "ha", flip))

    buffers = [adjoint_source, forward_field, other[0]] + own[1:] + other[1:]
    adjoint, gradient = pl.pallas_call(
        functools.partial(sweep_kernel, sz, mix_pairs.shape[1]),
        out_shape=[
            jax.ShapeDtypeStruct(adjoint_source.shape, f32),
            jax.ShapeDtypeStruct(permittivity.shape, f32),
        ],
        in_specs=[VMEM] * (2 + len(buffers)),
        out_specs=[VMEM] * 2,
        scratch_shapes=[
            field(sz.wide),
            field(sz.wide),
            field(sz.wide),
            field(sz.wide - 2),
            pltpu.VMEM((sz.harmonics, sz.wide, sz.halves, sz.rows, LANES), f32),
            pltpu.VMEM((2, sz.harmonics, 2, 3, sz.halves, sz.rows, LANES), f32),
            pltpu.VMEM((sz.wide, sz.halves, sz.rows, LANES), f32),
            pltpu.SMEM((SUBS, LANES), f32),
            pltpu.SemaphoreType.DMA,
        ],
        compiler_params=pltpu.CompilerParams(
            vmem_limit_bytes=32 * 1024 * 1024,
        ),
        name="sweeps",
    )(table, permittivity, *buffers)
    return (adjoint, gradient)


def solution(mesh):
    return jax.shard_map(
        shards,
        mesh=mesh,
        in_specs=(
            P("ha", None, None, ("cand", "gx"), "gy", None),
            P("ha", None, None, ("cand", "gx"), "gy", None),
            P(("cand", "gx"), "gy", None),
            P(),
            P(("cand", "gx"), "gy"),
            P(),
            P(),
        ),
        out_specs=(P("ha", None, None, ("cand", "gx"), "gy", None), P(("cand", "gx"), "gy", None)),
        check_vma=False,
    )
```
